32 devices in a mesh: groups: 2 (over y), seq: 4 (over z), section: 4 (over x, core).
Axes of the slice: x: 2, y: 2, z: 4, core: 2. Of those that a mesh axis runs over, the one named last changes fastest.
Arguments:
- hidden: bfloat16 [4, 32, 3072], P('section', ('groups', 'seq')), parts along dimension 1, may hold values from -6 to 6
- kv_cache: bfloat16 [4, 4, 32, 2, 3072], P('section', None, ('groups', 'seq')), parts along dimension 2, may hold values from -400 to 400
- w_qkv: bfloat16 [4, 3072, 3, 3072], P('section', None, None, 'seq'), may hold values from -0.109375 to 0.109375
- w_out: bfloat16 [4, 3072, 3072], P('section', None, 'seq'), may hold values from -0.109375 to 0.109375
- norm_gain: float32 [4, 2, 128], P('section'), may hold values from 1 to 2
- modulation: float32 [4, 4, 3, 3072], P('section'), may hold values from -5 to 5
- patch_order: int32 [8], P('groups'), parts along dimension 0, may hold values from 0 to 3, each once
- timestep: int32 [8], P('groups'), parts along dimension 0, may hold values from 0 to 3
Outputs:
- next_hidden: bfloat16 [4, 32, 3072], P('section', ('groups', 'seq')), parts along dimension 1
- fresh_kv: bfloat16 [4, 32, 2, 3072], P('section', ('groups', 'seq')), parts along dimension 1
The draws below stay inside these ranges and needn't reach their ends.
There are 2 independent parts, one for each index of `groups`. The reference program is written for one: setup_inputs(seed, part) draws one part's arguments, and reference() takes and returns one part's arrays. A program takes and returns all parts, laid end to end along the dimension named above; an argument that names none is the same for every part. Nothing has to cross between parts.
Inputs may be any that keep to these rules, and one draw needn't show every extreme that they name: `patch_order`: each section holds a different patch.
All inputs are finite; a program needn't handle non-finite values.
Results may differ from the reference program's by a relative error of at most 0.02.
The reference program's roundings to bfloat16 on the way count: a program that leaves them out, or rounds other values in their place, can miss the bound.
Values may be sent and summed in bfloat16 or wider, within the bound.
No kernel may reach another device: no remote copies, remote signals or barrier semaphores. Data moves between devices by JAX's collectives and lax.ppermute only.
A program may use at most 64 MiB of HBM per device.

```python
import math
import jax
import jax.numpy as jnp
from jax import lax

D = 3072
HEADS = 24
HEAD = 128
STEPS = 4
TOK_DEV = 4
PATCHES = 4
T_PATCH = 16
LENGTH = 64
N_SECTION = 4


def draw_kv_cache(key, part):
    key_a, key_b = jax.random.split(jax.random.fold_in(key, 11), 2)
    shape = (N_SECTION, PATCHES, T_PATCH, HEADS, HEAD)
    key_part = 1.5 * jax.random.normal(key_a, shape, jnp.float32)
    value_part = jax.random.normal(key_b, shape, jnp.float32)
    key_part = jnp.clip(key_part, -400.0, 400.0)
    stacked = jnp.stack([key_part.reshape(N_SECTION, PATCHES, T_PATCH, D), value_part.reshape(N_SECTION, PATCHES, T_PATCH, D)], axis=3)
    return stacked.astype(jnp.bfloat16)


def plant(array, key, smallest, top_value):
    place = [jax.random.randint(jax.random.fold_in(key, axis), (), 0, length) for axis, length in enumerate(array.shape)]
    widest = array.shape.index(max(array.shape))
    next_to = place[:widest] + [(place[widest] + 1) % array.shape[widest]] + place[widest + 1:]
    return array.at[tuple(place)].set(smallest).at[tuple(next_to)].set(top_value)


def levels(key, shape, pieces, smallest, high):
    level = 1.0
    for dim, blocks in pieces:
        draws = jax.random.uniform(jax.random.fold_in(jax.random.fold_in(key, 6), dim), (blocks,), jnp.float32, smallest / len(pieces), high / len(pieces))
        level = level * jnp.repeat(jnp.exp(draws), shape[dim] // blocks).reshape((-1,) + (1,) * (len(shape) - 1 - dim))
    return level


def gaussian(rng, extent, scale, bound, cuts=(), held_as=jnp.bfloat16):
    drawn = scale * jax.random.normal(rng, extent, jnp.float32)
    if cuts:
        drawn = drawn * levels(rng, extent, cuts, -0.22, 0.18)
    return jnp.clip(drawn, -bound, bound).astype(held_as)


def setup_inputs(seed: int = 0, part: int = 0) -> dict:
    seeds = jax.random.split(jax.random.key(seed), 9)
    part_splits = jax.random.split(jax.random.fold_in(seeds[8], part), 9)
    return {
        "hidden": gaussian(part_splits[0], (N_SECTION, T_PATCH, D), 1.0, 6.0, ((0, 4), (1, 4))),
        "kv_cache": draw_kv_cache(jax.random.fold_in(jax.random.fold_in(seeds[8], part), 71), part),
        "w_qkv": gaussian(seeds[2], (N_SECTION, D, 3, D), D ** -0.5, 0.109375, ((0, 4), (3, 4))),
        "w_out": gaussian(seeds[3], (N_SECTION, D, D), D ** -0.5, 0.109375, ((0, 4), (2, 4))),
        "norm_gain": jnp.clip(1.0 + 1.0 * jax.random.uniform(seeds[4], (N_SECTION, 2, HEAD), jnp.float32) ** levels(seeds[4], (N_SECTION, 2, HEAD), ((0, 4),), -0.2, 0.2), 1.0, 2.0),
        "modulation": gaussian(seeds[5], (N_SECTION, STEPS, 3, D), 1.0, 5.0, ((0, 4),), jnp.float32),
        "patch_order": jax.random.permutation(part_splits[6], N_SECTION).astype(jnp.int32),
        "timestep": plant(jax.random.randint(part_splits[7], (N_SECTION,), 0, STEPS), jax.random.fold_in(part_splits[7], 1), 0, STEPS - 1).astype(jnp.int32),
    }


def layer_norm(values_in):
    center = values_in - lax.optimization_barrier(jnp.mean(values_in, axis=-1, keepdims=True))
    spread = lax.optimization_barrier(jnp.mean(center * center, axis=-1, keepdims=True))
    return center * lax.rsqrt(spread + 1e-06)

def head_norm(values_in, gain):
    square = lax.optimization_barrier(jnp.mean(values_in * values_in, axis=-1, keepdims=True))
    return values_in * lax.rsqrt(square + 1e-06) * gain

def section_block(hidden, cache, w_qkv, w_out, norm_gain, modulation, patch_index, step_index):
    modulate = lax.dynamic_index_in_dim(modulation, step_index.astype(jnp.int32), 0, keepdims=False)
    rows_in = hidden.astype(jnp.float32)
    normed = (layer_norm(rows_in) * (1.0 + modulate[1]) + modulate[0]).astype(jnp.bfloat16)
    projected = jnp.dot(normed, w_qkv.reshape(D, 3 * D), preferred_element_type=jnp.float32).astype(jnp.bfloat16)
    projected = projected.reshape(T_PATCH, 3, HEADS, HEAD)
    queries = head_norm(projected[:, 0].astype(jnp.float32), norm_gain[0]).astype(jnp.bfloat16)
    key_rows = head_norm(projected[:, 1].astype(jnp.float32), norm_gain[1]).astype(jnp.bfloat16)
    fresh = jnp.stack([key_rows.reshape(T_PATCH, D), projected[:, 2].reshape(T_PATCH, D)], axis=1)
    zero = jnp.zeros((), jnp.int32)
    merged = lax.dynamic_update_slice(cache, fresh[None], (patch_index.astype(jnp.int32), zero, zero, zero))
    group_count = T_PATCH // TOK_DEV
    all_keys = merged[:, :, 0].reshape(LENGTH, HEADS, HEAD).astype(jnp.float32)
    all_values = merged[:, :, 1].reshape(PATCHES, group_count, TOK_DEV, HEADS, HEAD).astype(jnp.float32)
    scores = jnp.einsum('thd,shd->hts', queries.astype(jnp.float32), all_keys) / math.sqrt(HEAD)
    top = lax.optimization_barrier(jnp.max(scores, axis=-1, keepdims=True))
    rounded = jnp.exp(scores - top).astype(jnp.bfloat16)
    weights = lax.optimization_barrier(rounded).astype(jnp.float32)
    weights = weights.reshape(HEADS, T_PATCH, PATCHES, group_count, TOK_DEV)
    partial_den = lax.optimization_barrier(jnp.sum(weights, axis=(2, 4))).astype(jnp.bfloat16)
    denominator = lax.optimization_barrier(jnp.sum(lax.optimization_barrier(partial_den).astype(jnp.float32), axis=-1))
    partial_num = jnp.einsum('htpgk,pgkhd->gthd', weights, all_values).astype(jnp.bfloat16)
    numerator = lax.optimization_barrier(jnp.sum(lax.optimization_barrier(partial_num).astype(jnp.float32), axis=0))
    attention = (numerator / denominator.T[:, :, None]).astype(jnp.bfloat16).reshape(T_PATCH, D)
    attn_out = jnp.dot(attention, w_out, preferred_element_type=jnp.float32).astype(jnp.bfloat16)
    block = (rows_in + modulate[2] * attn_out.astype(jnp.float32)).astype(jnp.bfloat16)
    return (block, fresh)

def reference(hidden, kv_cache, w_qkv, w_out, norm_gain, modulation, patch_order, timestep):

    def one_section(packed):
        return section_block(*packed)
    blocks, fresh_kv = lax.map(one_section, (hidden, kv_cache, w_qkv, w_out, norm_gain, modulation, patch_order, timestep))
    next_hidden = jnp.roll(blocks, 1, axis=0)
    return (next_hidden, fresh_kv)
```

```python
import functools
import math

import jax
import jax.numpy as jnp
from jax import lax
from jax.experimental import pallas as pl
from jax.experimental.pallas import tpu as pltpu
from jax.sharding import PartitionSpec as P


F32 = jnp.float32
BF16 = jnp.bfloat16
VMEM = pl.BlockSpec(memory_space=pltpu.VMEM)
SMEM = pl.BlockSpec(memory_space=pltpu.SMEM)
HBM = pl.BlockSpec(memory_space=pl.ANY)


def passed_along(array, axis, by):
    count = lax.axis_size(axis)
    return lax.ppermute(array, axis, [(i, (i + by) % count) for i in range(count)])


def layer_norm(values_in):
    center = values_in - jnp.mean(values_in, axis=-1, keepdims=True)
    spread = jnp.mean(center * center, axis=-1, keepdims=True)
    return center * lax.rsqrt(spread + 1e-06)


def head_norm(values_in, gain):
    square = jnp.mean(values_in * values_in, axis=-1, keepdims=True)
    return values_in * lax.rsqrt(square + 1e-06) * gain


def swapped(slots, number):
    return jnp.concatenate([slots[b ^ number] for b in range(len(slots))], axis=0)


def pack_kernel(order_ref, cache_ref, *refs, slots, tokens, patches, columns):
    outs, held, sems = refs[:slots], refs[slots], refs[slots + 1]
    mine = lax.axis_index("seq")
    patch = order_ref[lax.axis_index("section")]
    copies = []
    for i in range(patches - 1):
        stale = lax.rem(patch + (i + 1), patches)
        copies.append(pltpu.make_async_copy(cache_ref.at[0, stale], held.at[i], sems.at[i]))
    for copy in copies:
        copy.start()
    for copy in copies:
        copy.wait()
    rows = (patches - 1) * tokens
    for b in range(slots):
        start = pl.multiple_of((mine ^ b) * columns, columns)
        both = held[:, :, :, pl.ds(start, columns)].astype(F32)
        both = both.reshape(rows, 2, columns)
        outs[b][...] = jnp.concatenate([both[:, 0], both[:, 1]], axis=0).astype(BF16)


def project_kernel(step_ref, mod_ref, gain_ref, weight_ref, *refs, slots, tokens, heads, size):
    hidden = [r[...] for r in refs[:slots]]
    q_ref, held_ref, gate_ref = refs[slots : slots + 3]
    fresh_refs = refs[slots + 3 : 2 * slots + 3]
    mine = lax.axis_index("seq")
    step = step_ref[lax.axis_index("section")]
    columns = heads * size
    shift = mod_ref[0, pl.ds(step, 1), :]
    scale = mod_ref[1, pl.ds(step, 1), :]
    start = pl.multiple_of(mine * columns, columns)
    gate_ref[...] = mod_ref[2, pl.ds(step, 1), pl.ds(start, columns)]
    for b in range(slots):
        held_ref[b] = refs[b][:, pl.ds(start, columns)]
    rows = jnp.concatenate([h.astype(F32) for h in hidden], axis=0)
    normed = (layer_norm(rows) * (1.0 + scale) + shift).astype(BF16)
    parts = []
    for part in range(3):
        dotted = jnp.dot(normed, weight_ref[part], preferred_element_type=F32)
        parts.append(dotted.astype(BF16).astype(F32))
    normed_heads = []
    for part in range(2):
        gain = gain_ref[pl.ds(part, 1), :]
        normed_heads.append(
            jnp.concatenate(
                [head_norm(parts[part][:, h * size : (h + 1) * size], gain) for h in range(heads)], axis=1
            )
        )
    q_ref[...] = normed_heads[0].astype(BF16)
    keys, values = normed_heads[1], parts[2]
    for b in range(slots):
        own = slice(b * tokens, (b + 1) * tokens)
        fresh_refs[b][...] = jnp.concatenate([keys[own], values[own]], axis=0).astype(BF16)


def attend_kernel(q_ref, *refs, slots, tokens, stale, heads, size):
    fresh, old = refs[:slots], refs[slots : 2 * slots]
    outs = refs[2 * slots : 3 * slots]
    per = stale + tokens
    fresh = [r[...].astype(F32) for r in fresh]
    old = [r[...].astype(F32) for r in old]
    keys = jnp.concatenate([x for b in range(slots) for x in (old[b][:stale], fresh[b][:tokens])], axis=0).astype(BF16)
    values = jnp.concatenate([x for b in range(slots) for x in (old[b][stale:], fresh[b][tokens:])], axis=0).astype(BF16)
    count = slots * per
    queries = q_ref[...]
    length = queries.shape[0]
    lane = lax.broadcasted_iota(jnp.int32, (length, count), 1)
    ones = jnp.ones((count, size), BF16)
    rows = []
    for h in range(heads):
        cut = slice(h * size, (h + 1) * size)
        scores = lax.dot_general(
            queries[:, cut], keys[:, cut], (((1,), (1,)), ((), ())), preferred_element_type=F32
        ) / math.sqrt(size)
        top = jnp.max(scores, axis=-1, keepdims=True)
        weights = jnp.exp(scores - top).astype(BF16).astype(F32)
        apart = jnp.concatenate(
            [jnp.where((lane >= b * per) & (lane < (b + 1) * per), weights, 0.0) for b in range(slots)], axis=0
        ).astype(BF16)
        both = jnp.dot(apart, jnp.concatenate([values[:, cut], ones], axis=1), preferred_element_type=F32)
        both = both.astype(BF16).astype(F32)
        total = both[:length]
        for b in range(1, slots):
            total = total + both[b * length : (b + 1) * length]
        rows.append(total[:, :size] / total[:, size:])
    rows = jnp.concatenate(rows, axis=1)
    pieces = [rows[b * tokens : (b + 1) * tokens] for b in range(slots)]
    for b in range(slots):
        outs[b][...] = swapped(pieces, b).astype(BF16)


def output_kernel(gate_ref, held_ref, weight_ref, *refs, slots, tokens):
    columns = weight_ref.shape[1]
    mine = lax.axis_index("seq")
    total = None
    for b in range(slots):
        start = pl.multiple_of((mine ^ b) * columns, columns)
        term = jnp.dot(refs[b][...], weight_ref[pl.ds(start, columns), :], preferred_element_type=F32)
        total = term if total is None else total + term
    out = total.astype(BF16).astype(F32)
    gate = gate_ref[...]
    for b in range(slots):
        piece = held_ref[b].astype(F32) + gate * out[b * tokens : (b + 1) * tokens]
        refs[slots + b][...] = piece.astype(BF16)


def place_kernel(*refs, slots):
    out_ref = refs[slots]
    columns = refs[0].shape[1]
    mine = lax.axis_index("seq")
    for b in range(slots):
        start = pl.multiple_of((mine ^ b) * columns, columns)
        out_ref[0, :, pl.ds(start, columns)] = refs[b][...]


def place_kv_kernel(*refs, slots, tokens):
    out_ref = refs[slots]
    columns = refs[0].shape[1]
    mine = lax.axis_index("seq")
    for b in range(slots):
        start = pl.multiple_of((mine ^ b) * columns, columns)
        piece = refs[b][...].astype(F32)
        both = jnp.stack([piece[:tokens], piece[tokens:]], axis=1)
        out_ref[0, :, :, pl.ds(start, columns)] = both.astype(BF16)


def body_by_heads(hidden, kv_cache, w_qkv, w_out, norm_gain, modulation, patch_order, timestep):
    slots, sections = lax.axis_size("seq"), lax.axis_size("section")
    tokens, width = hidden.shape[1:]
    patches = kv_cache.shape[1]
    columns, size = w_qkv.shape[3], norm_gain.shape[2]
    heads, stale = columns // size, (patches - 1) * tokens
    params = pltpu.CompilerParams(vmem_limit_bytes=16 * 2**20)
    shape = jax.ShapeDtypeStruct

    def swap(array, number):
        return lax.ppermute(array, "seq", [(i, i ^ number) for i in range(slots)])

    own = hidden[0]
    rows = [own] + [swap(own, b) for b in range(1, slots)]
    packed = pl.pallas_call(
        functools.partial(pack_kernel, slots=slots, tokens=tokens, patches=patches, columns=columns),
        out_shape=[shape((2 * stale, columns), BF16)] * slots,
        in_specs=[SMEM, HBM],
        out_specs=[VMEM] * slots,
        scratch_shapes=[
            pltpu.VMEM((patches - 1, tokens, 2, width), BF16),
            pltpu.SemaphoreType.DMA((patches - 1,)),
        ],
        compiler_params=params,
        name="pack",
    )(patch_order, kv_cache)
    old = [packed[0]] + [swap(packed[b], b) for b in range(1, slots)]
    queries, held, gate, *fresh = pl.pallas_call(
        functools.partial(project_kernel, slots=slots, tokens=tokens, heads=heads, size=size),
        out_shape=[
            shape((slots * tokens, columns), BF16),
            shape((slots, tokens, columns), BF16),
            shape((1, columns), F32),
        ]
        + [shape((2 * tokens, columns), BF16)] * slots,
        in_specs=[SMEM] + [VMEM] * (3 + slots),
        out_specs=[VMEM] * (3 + slots),
        compiler_params=params,
        name="project",
    )(
        timestep,
        jnp.transpose(modulation[0], (1, 0, 2)),
        norm_gain[0],
        jnp.transpose(w_qkv[0], (1, 0, 2)),
        *rows,
    )
    ordered = pl.pallas_call(
        functools.partial(attend_kernel, slots=slots, tokens=tokens, stale=stale, heads=heads, size=size),
        out_shape=[shape((slots * tokens, columns), BF16)] * slots,
        in_specs=[VMEM] * (1 + 2 * slots),
        out_specs=[VMEM] * slots,
        compiler_params=params,
        name="attend",
    )(queries, *fresh, *old)
    attention = [ordered[0]] + [swap(ordered[b], b) for b in range(1, slots)]
    pieces = pl.pallas_call(
        functools.partial(output_kernel, slots=slots, tokens=tokens),
        out_shape=[shape((tokens, columns), BF16)] * slots,
        in_specs=[VMEM] * (3 + slots),
        out_specs=[VMEM] * slots,
        compiler_params=params,
        name="output",
    )(gate, held, w_out[0], *attention)

    def onward(array, number):
        pairs = [
            (j * sections + s, (j ^ number) * sections + (s + 1) % sections)
            for j in range(slots)
            for s in range(sections)
        ]
        return lax.ppermute(array, ("seq", "section"), pairs)

    arrived = [onward(pieces[b], b) for b in range(slots)]
    fresh_here = [fresh[0]] + [swap(fresh[b], b) for b in range(1, slots)]
    fresh_kv = pl.pallas_call(
        functools.partial(place_kv_kernel, slots=slots, tokens=tokens),
        out_shape=shape((1, tokens, 2, width), BF16),
        in_specs=[VMEM] * slots,
        out_specs=VMEM,
        compiler_params=params,
        name="place_kv",
    )(*fresh_here)
    next_hidden = pl.pallas_call(
        functools.partial(place_kernel, slots=slots),
        out_shape=shape((1, tokens, width), BF16),
        in_specs=[VMEM] * slots,
        out_specs=VMEM,
        compiler_params=params,
        name="place",
    )(*arrived)
    return (next_hidden, fresh_kv)


def body_by_tokens(hidden, kv_cache, w_qkv, w_out, norm_gain, modulation, patch_order, timestep):
    section_index = lax.axis_index("section")
    patch_index = lax.dynamic_index_in_dim(patch_order, section_index, 0, keepdims=False)
    step_index = lax.dynamic_index_in_dim(timestep, section_index, 0, keepdims=False)
    modulate = lax.dynamic_index_in_dim(modulation[0], step_index, 0, keepdims=False)
    model_width = hidden.shape[2]
    head_size = norm_gain.shape[2]
    head_count = model_width // head_size
    col_width = w_qkv.shape[3]
    rows_in = hidden[0].astype(jnp.float32)
    own_count = rows_in.shape[0]
    normed = (layer_norm(rows_in) * (1.0 + modulate[1]) + modulate[0]).astype(jnp.bfloat16)
    w_local = w_qkv[0].reshape(model_width, 3 * col_width)
    projected = jnp.dot(
        lax.all_gather(normed, "seq", axis=0, tiled=True),
        w_local,
        preferred_element_type=jnp.float32,
    ).astype(jnp.bfloat16)
    patch_len = projected.shape[0]
    projected = projected.reshape(patch_len, 3, col_width)
    query_cols = lax.all_gather(projected[:, 0], "seq", axis=1, tiled=True)
    kv_rows = lax.all_to_all(projected[:, 1:], "seq", split_axis=0, concat_axis=2, tiled=True)
    queries = head_norm(
        query_cols.astype(jnp.float32).reshape(patch_len, head_count, head_size), norm_gain[0, 0]
    ).astype(jnp.bfloat16)
    key_rows = head_norm(
        kv_rows[:, 0].astype(jnp.float32).reshape(own_count, head_count, head_size), norm_gain[0, 1]
    ).astype(jnp.bfloat16)
    fresh = jnp.stack([key_rows.reshape(own_count, model_width), kv_rows[:, 1]], axis=1)
    zero = jnp.zeros((), jnp.int32)
    local_kv = lax.dynamic_update_slice(kv_cache[0], fresh[None], (patch_index, zero, zero, zero))
    patch_count = local_kv.shape[0]
    local_keys = local_kv[:, :, 0].reshape(patch_count * own_count, head_count, head_size)
    local_values = local_kv[:, :, 1].reshape(patch_count * own_count, head_count, head_size)
    scores = jnp.einsum(
        "thd,shd->hts", queries, local_keys, preferred_element_type=jnp.float32
    ) / math.sqrt(head_size)
    row_top = lax.pmax(jnp.max(scores, axis=-1), "seq")
    weights = jnp.exp(scores - row_top[:, :, None]).astype(jnp.bfloat16)
    denominator = jnp.sum(weights, axis=-1, dtype=jnp.float32).T
    numerator = jnp.einsum(
        "hts,shd->thd", weights, local_values, preferred_element_type=jnp.float32
    ).reshape(patch_len, model_width)
    totals, counts = (
        lax.psum(numerator.astype(jnp.bfloat16), "seq").astype(jnp.float32),
        lax.psum(denominator.astype(jnp.bfloat16), "seq").astype(jnp.float32),
    )
    attention = (totals.reshape(patch_len, head_count, head_size) / counts[:, :, None]).astype(
        jnp.bfloat16
    )
    attention = attention.reshape(patch_len, model_width)
    out_cols = jnp.dot(attention, w_out[0], preferred_element_type=jnp.float32).astype(jnp.bfloat16)
    out_rows = lax.all_to_all(out_cols, "seq", split_axis=0, concat_axis=1, tiled=True)
    block = (rows_in + modulate[2] * out_rows.astype(jnp.float32)).astype(jnp.bfloat16)
    arrived = passed_along(block, "section", 1)
    return (arrived[None], fresh[None])


def body(hidden, kv_cache, w_qkv, w_out, norm_gain, modulation, patch_order, timestep):
    count = lax.axis_size("seq")
    whole_heads = w_qkv.shape[3] % norm_gain.shape[2] == 0
    chosen = body_by_heads if whole_heads and count & (count - 1) == 0 else body_by_tokens
    return chosen(hidden, kv_cache, w_qkv, w_out, norm_gain, modulation, patch_order, timestep)


def solution(mesh):
    return jax.shard_map(
        body,
        mesh=mesh,
        in_specs=(
            P("section", ("groups", "seq"), None),
            P("section", None, ("groups", "seq"), None, None),
            P("section", None, None, "seq"),
            P("section", None, "seq"),
            P("section", None, None),
            P("section", None, None, None),
            P("groups"),
            P("groups"),
        ),
        out_specs=(
            P("section", ("groups", "seq"), None),
            P("section", ("groups", "seq"), None, None),
        ),
        check_vma=False,
    )
```

```python
import functools
import math

import jax
import jax.numpy as jnp
from jax import lax
from jax.experimental import pallas as pl
from jax.experimental.pallas import tpu as pltpu
from jax.sharding import PartitionSpec as P


F32 = jnp.float32
BF16 = jnp.bfloat16
VMEM = pl.BlockSpec(memory_space=pltpu.VMEM)
SMEM = pl.BlockSpec(memory_space=pltpu.SMEM)
HBM = pl.BlockSpec(memory_space=pl.ANY)


def passed_along(array, axis, by):
    count = lax.axis_size(axis)
    return lax.ppermute(array, axis, [(i, (i + by) % count) for i in range(count)])


def layer_norm(values_in):
    center = values_in - jnp.mean(values_in, axis=-1, keepdims=True)
    spread = jnp.mean(center * center, axis=-1, keepdims=True)
    return center * lax.rsqrt(spread + 1e-06)


def head_norm(values_in, gain):
    square = jnp.mean(values_in * values_in, axis=-1, keepdims=True)
    return values_in * lax.rsqrt(square + 1e-06) * gain


def cost(flops):
    return pl.CostEstimate(flops=int(flops), transcendentals=0, bytes_accessed=2**20)


def swapped(slots, number):
    return jnp.concatenate([slots[b ^ number] for b in range(len(slots))], axis=0)


def pack_kernel(order_ref, cache_ref, *refs, slots, tokens, patches, columns):
    outs, held, sems = refs[:slots], refs[slots], refs[slots + 1]
    mine = lax.axis_index("seq")
    patch = order_ref[lax.axis_index("section")]
    copies = []
    for i in range(patches - 1):
        stale = lax.rem(patch + (i + 1), patches)
        copies.append(pltpu.make_async_copy(cache_ref.at[0, stale], held.at[i], sems.at[i]))
    for copy in copies:
        copy.start()
    for copy in copies:
        copy.wait()
    rows = (patches - 1) * tokens
    for b in range(slots):
        start = pl.multiple_of((mine ^ b) * columns, columns)
        both = held[:, :, :, pl.ds(start, columns)].astype(F32)
        both = both.reshape(rows, 2, columns)
        outs[b][...] = jnp.concatenate([both[:, 0], both[:, 1]], axis=0).astype(BF16)


def project_kernel(step_ref, mod_ref, gain_ref, weight_ref, *refs, slots, tokens, heads, size):
    hidden_refs = refs[:slots][::-1]
    q_ref, held_ref, gate_ref = refs[slots : slots + 3]
    fresh_refs = refs[slots + 3 : 2 * slots + 3]
    mine = lax.axis_index("seq")
    step = step_ref[lax.axis_index("section")]
    columns = heads * size
    shift = mod_ref[0, pl.ds(step, 1), :]
    scale = mod_ref[1, pl.ds(step, 1), :]
    start = pl.multiple_of(mine * columns, columns)
    gate_ref[...] = mod_ref[2, pl.ds(step, 1), pl.ds(start, columns)]
    for b in range(slots):
        held_ref[b] = hidden_refs[b][:, pl.ds(start, columns)]
    rows = jnp.concatenate([r[...].astype(F32) for r in hidden_refs], axis=0)
    normed = (layer_norm(rows) * (1.0 + scale) + shift).astype(BF16)
    parts = []
    for part in range(3):
        dotted = jnp.dot(normed, weight_ref[part], preferred_element_type=F32)
        parts.append(dotted.astype(BF16).astype(F32))
    normed_heads = []
    for part in range(2):
        gain = gain_ref[pl.ds(part, 1), :]
        normed_heads.append(
            jnp.concatenate(
                [head_norm(parts[part][:, h * size : (h + 1) * size], gain) for h in range(heads)], axis=1
            )
        )
    q_ref[...] = normed_heads[0].astype(BF16)
    keys, values = normed_heads[1], parts[2]
    for b in range(slots):
        own = slice(b * tokens, (b + 1) * tokens)
        fresh_refs[b][...] = jnp.concatenate([keys[own], values[own]], axis=0).astype(BF16)


def attend_kernel(q_ref, *refs, slots, tokens, stale, heads, size):
    fresh, old = refs[:slots], refs[slots : 2 * slots][::-1]
    outs = refs[2 * slots : 3 * slots]
    per = stale + tokens
    fresh = [r[...].astype(F32) for r in fresh]
    old = [r[...].astype(F32) for r in old]
    keys = jnp.concatenate([x for b in range(slots) for x in (old[b][:stale], fresh[b][:tokens])], axis=0).astype(BF16)
    values = jnp.concatenate([x for b in range(slots) for x in (old[b][stale:], fresh[b][tokens:])], axis=0).astype(BF16)
    count = slots * per
    queries = q_ref[...]
    length = queries.shape[0]
    lane = lax.broadcasted_iota(jnp.int32, (length, count), 1)
    ones = jnp.ones((count, size), BF16)
    rows = []
    for h in range(heads):
        cut = slice(h * size, (h + 1) * size)
        scores = lax.dot_general(
            queries[:, cut], keys[:, cut], (((1,), (1,)), ((), ())), preferred_element_type=F32
        ) / math.sqrt(size)
        top = jnp.max(scores, axis=-1, keepdims=True)
        weights = jnp.exp(scores - top).astype(BF16).astype(F32)
        apart = jnp.concatenate(
            [jnp.where((lane >= b * per) & (lane < (b + 1) * per), weights, 0.0) for b in range(slots)], axis=0
        ).astype(BF16)
        both = jnp.dot(apart, jnp.concatenate([values[:, cut], ones], axis=1), preferred_element_type=F32)
        both = both.astype(BF16).astype(F32)
        total = both[:length]
        for b in range(1, slots):
            total = total + both[b * length : (b + 1) * length]
        rows.append(total[:, :size] / total[:, size:])
    rows = jnp.concatenate(rows, axis=1)
    pieces = [rows[b * tokens : (b + 1) * tokens] for b in range(slots)]
    for b in range(slots):
        outs[b][...] = swapped(pieces, b).astype(BF16)


def output_kernel(gate_ref, held_ref, weight_ref, *refs, slots, tokens):
    columns = weight_ref.shape[1]
    attention = refs[:slots][::-1]
    mine = lax.axis_index("seq")
    total = None
    for b in range(slots):
        start = pl.multiple_of((mine ^ b) * columns, columns)
        term = jnp.dot(attention[b][...], weight_ref[pl.ds(start, columns), :], preferred_element_type=F32)
        total = term if total is None else total + term
    out = total.astype(BF16).astype(F32)
    gate = gate_ref[...]
    for b in range(slots):
        piece = held_ref[b].astype(F32) + gate * out[b * tokens : (b + 1) * tokens]
        refs[slots + b][...] = piece.astype(BF16)


def place_kernel(*refs, slots):
    out_ref, refs = refs[slots], refs[:slots][::-1]
    columns = refs[0].shape[1]
    mine = lax.axis_index("seq")
    for b in range(slots):
        start = pl.multiple_of((mine ^ b) * columns, columns)
        out_ref[0, :, pl.ds(start, columns)] = refs[b][...]


def place_kv_kernel(*refs, slots, tokens):
    out_ref, refs = refs[slots], refs[:slots][::-1]
    columns = refs[0].shape[1]
    mine = lax.axis_index("seq")
    for b in range(slots):
        start = pl.multiple_of((mine ^ b) * columns, columns)
        piece = refs[b][...].astype(F32)
        both = jnp.stack([piece[:tokens], piece[tokens:]], axis=1)
        out_ref[0, :, :, pl.ds(start, columns)] = both.astype(BF16)


def body_by_heads(hidden, kv_cache, w_qkv, w_out, norm_gain, modulation, patch_order, timestep):
    slots, sections = lax.axis_size("seq"), lax.axis_size("section")
    tokens, width = hidden.shape[1:]
    patches = kv_cache.shape[1]
    columns, size = w_qkv.shape[3], norm_gain.shape[2]
    heads, stale = columns // size, (patches - 1) * tokens
    params = pltpu.CompilerParams(vmem_limit_bytes=16 * 2**20)
    shape = jax.ShapeDtypeStruct

    def swap(array, number):
        return lax.ppermute(array, "seq", [(i, i ^ number) for i in range(slots)])

    def swap_all(arrays):
        moved = {b: swap(arrays[b], b) for b in range(slots - 1, 0, -1)}
        return [arrays[0]] + [moved[b] for b in range(1, slots)]

    rows = swap_all([hidden[0]] * slots)
    packed = pl.pallas_call(
        functools.partial(pack_kernel, slots=slots, tokens=tokens, patches=patches, columns=columns),
        out_shape=[shape((2 * stale, columns), BF16)] * slots,
        in_specs=[SMEM, HBM],
        out_specs=[VMEM] * slots,
        scratch_shapes=[
            pltpu.VMEM((patches - 1, tokens, 2, width), BF16),
            pltpu.SemaphoreType.DMA((patches - 1,)),
        ],
        compiler_params=params,
        cost_estimate=cost(5e9),
        name="pack",
    )(patch_order, kv_cache)
    old = swap_all(packed)
    queries, held, gate, *fresh = pl.pallas_call(
        functools.partial(project_kernel, slots=slots, tokens=tokens, heads=heads, size=size),
        out_shape=[
            shape((slots * tokens, columns), BF16),
            shape((slots, tokens, columns), BF16),
            shape((1, columns), F32),
        ]
        + [shape((2 * tokens, columns), BF16)] * slots,
        in_specs=[SMEM] + [VMEM] * (3 + slots),
        out_specs=[VMEM] * (3 + slots),
        compiler_params=params,
        cost_estimate=cost(2e9),
        name="project",
    )(
        timestep,
        jnp.transpose(modulation[0], (1, 0, 2)),
        norm_gain[0],
        jnp.transpose(w_qkv[0], (1, 0, 2)),
        *rows[::-1],
    )
    ordered = pl.pallas_call(
        functools.partial(attend_kernel, slots=slots, tokens=tokens, stale=stale, heads=heads, size=size),
        out_shape=[shape((slots * tokens, columns), BF16)] * slots,
        in_specs=[VMEM] * (1 + 2 * slots),
        out_specs=[VMEM] * slots,
        compiler_params=params,
        cost_estimate=cost(2e9),
        name="attend",
    )(queries, *fresh, *old[::-1])
    attention = swap_all(ordered)
    pieces = pl.pallas_call(
        functools.partial(output_kernel, slots=slots, tokens=tokens),
        out_shape=[shape((tokens, columns), BF16)] * slots,
        in_specs=[VMEM] * (3 + slots),
        out_specs=[VMEM] * slots,
        compiler_params=params,
        cost_estimate=cost(2e9),
        name="output",
    )(gate, held, w_out[0], *attention[::-1])

    def onward(array, number):
        pairs = [
            (j * sections + s, (j ^ number) * sections + (s + 1) % sections)
            for j in range(slots)
            for s in range(sections)
        ]
        return lax.ppermute(array, ("seq", "section"), pairs)

    arrived = [onward(pieces[b], b) for b in range(slots - 1, -1, -1)][::-1]
    fresh_here = swap_all(fresh)
    fresh_kv = pl.pallas_call(
        functools.partial(place_kv_kernel, slots=slots, tokens=tokens),
        out_shape=shape((1, tokens, 2, width), BF16),
        in_specs=[VMEM] * slots,
        out_specs=VMEM,
        compiler_params=params,
        cost_estimate=cost(1e9),
        name="place_kv",
    )(*fresh_here[::-1])
    next_hidden = pl.pallas_call(
        functools.partial(place_kernel, slots=slots),
        out_shape=shape((1, tokens, width), BF16),
        in_specs=[VMEM] * slots,
        out_specs=VMEM,
        compiler_params=params,
        cost_estimate=cost(1e9),
        name="place",
    )(*arrived[::-1])
    return (next_hidden, fresh_kv)


def body_by_tokens(hidden, kv_cache, w_qkv, w_out, norm_gain, modulation, patch_order, timestep):
    section_index = lax.axis_index("section")
    patch_index = lax.dynamic_index_in_dim(patch_order, section_index, 0, keepdims=False)
    step_index = lax.dynamic_index_in_dim(timestep, section_index, 0, keepdims=False)
    modulate = lax.dynamic_index_in_dim(modulation[0], step_index, 0, keepdims=False)
    model_width = hidden.shape[2]
    head_size = norm_gain.shape[2]
    head_count = model_width // head_size
    col_width = w_qkv.shape[3]
    rows_in = hidden[0].astype(jnp.float32)
    own_count = rows_in.shape[0]
    normed = (layer_norm(rows_in) * (1.0 + modulate[1]) + modulate[0]).astype(jnp.bfloat16)
    w_local = w_qkv[0].reshape(model_width, 3 * col_width)
    projected = jnp.dot(
        lax.all_gather(normed, "seq", axis=0, tiled=True),
        w_local,
        preferred_element_type=jnp.float32,
    ).astype(jnp.bfloat16)
    patch_len = projected.shape[0]
    projected = projected.reshape(patch_len, 3, col_width)
    query_cols = lax.all_gather(projected[:, 0], "seq", axis=1, tiled=True)
    kv_rows = lax.all_to_all(projected[:, 1:], "seq", split_axis=0, concat_axis=2, tiled=True)
    queries = head_norm(
        query_cols.astype(jnp.float32).reshape(patch_len, head_count, head_size), norm_gain[0, 0]
    ).astype(jnp.bfloat16)
    key_rows = head_norm(
        kv_rows[:, 0].astype(jnp.float32).reshape(own_count, head_count, head_size), norm_gain[0, 1]
    ).astype(jnp.bfloat16)
    fresh = jnp.stack([key_rows.reshape(own_count, model_width), kv_rows[:, 1]], axis=1)
    zero = jnp.zeros((), jnp.int32)
    local_kv = lax.dynamic_update_slice(kv_cache[0], fresh[None], (patch_index, zero, zero, zero))
    patch_count = local_kv.shape[0]
    local_keys = local_kv[:, :, 0].reshape(patch_count * own_count, head_count, head_size)
    local_values = local_kv[:, :, 1].reshape(patch_count * own_count, head_count, head_size)
    scores = jnp.einsum(
        "thd,shd->hts", queries, local_keys, preferred_element_type=jnp.float32
    ) / math.sqrt(head_size)
    row_top = lax.pmax(jnp.max(scores, axis=-1), "seq")
    weights = jnp.exp(scores - row_top[:, :, None]).astype(jnp.bfloat16)
    denominator = jnp.sum(weights, axis=-1, dtype=jnp.float32).T
    numerator = jnp.einsum(
        "hts,shd->thd", weights, local_values, preferred_element_type=jnp.float32
    ).reshape(patch_len, model_width)
    totals, counts = (
        lax.psum(numerator.astype(jnp.bfloat16), "seq").astype(jnp.float32),
        lax.psum(denominator.astype(jnp.bfloat16), "seq").astype(jnp.float32),
    )
    attention = (totals.reshape(patch_len, head_count, head_size) / counts[:, :, None]).astype(
        jnp.bfloat16
    )
    attention = attention.reshape(patch_len, model_width)
    out_cols = jnp.dot(attention, w_out[0], preferred_element_type=jnp.float32).astype(jnp.bfloat16)
    out_rows = lax.all_to_all(out_cols, "seq", split_axis=0, concat_axis=1, tiled=True)
    block = (rows_in + modulate[2] * out_rows.astype(jnp.float32)).astype(jnp.bfloat16)
    arrived = passed_along(block, "section", 1)
    return (arrived[None], fresh[None])


def body(hidden, kv_cache, w_qkv, w_out, norm_gain, modulation, patch_order, timestep):
    count = lax.axis_size("seq")
    whole_heads = w_qkv.shape[3] % norm_gain.shape[2] == 0
    chosen = body_by_heads if whole_heads and count & (count - 1) == 0 else body_by_tokens
    return chosen(hidden, kv_cache, w_qkv, w_out, norm_gain, modulation, patch_order, timestep)


def solution(mesh):
    return jax.shard_map(
        body,
        mesh=mesh,
        in_specs=(
            P("section", ("groups", "seq"), None),
            P("section", None, ("groups", "seq"), None, None),
            P("section", None, None, "seq"),
            P("section", None, "seq"),
            P("section", None, None),
            P("section", None, None, None),
            P("groups"),
            P("groups"),
        ),
        out_specs=(
            P("section", ("groups", "seq"), None),
            P("section", ("groups", "seq"), None, None),
        ),
        check_vma=False,
    )
```

```python
import functools
import math

import jax
import jax.numpy as jnp
from jax import lax
from jax.experimental import pallas as pl
from jax.experimental.pallas import tpu as pltpu
from jax.sharding import PartitionSpec as P


F32 = jnp.float32
BF16 = jnp.bfloat16
VMEM = pl.BlockSpec(memory_space=pltpu.VMEM)
SMEM = pl.BlockSpec(memory_space=pltpu.SMEM)
HBM = pl.BlockSpec(memory_space=pl.ANY)


def passed_along(array, axis, by):
    count = lax.axis_size(axis)
    return lax.ppermute(array, axis, [(i, (i + by) % count) for i in range(count)])


def layer_norm(values_in):
    center = values_in - jnp.mean(values_in, axis=-1, keepdims=True)
    spread = jnp.mean(center * center, axis=-1, keepdims=True)
    return center * lax.rsqrt(spread + 1e-06)


def head_norm(values_in, gain):
    square = jnp.mean(values_in * values_in, axis=-1, keepdims=True)
    return values_in * lax.rsqrt(square + 1e-06) * gain


def cost(flops):
    return pl.CostEstimate(flops=int(flops), transcendentals=0, bytes_accessed=2**20)


def swapped(slots, number):
    return jnp.concatenate([slots[b ^ number] for b in range(len(slots))], axis=0)


def ahead_kernel(out_ref):
    out_ref[...] = jnp.zeros_like(out_ref)


def pack_kernel(order_ref, _, cache_ref, *refs, slots, tokens, patches, columns):
    outs, held, sems = refs[:slots], refs[slots], refs[slots + 1]
    mine = lax.axis_index("seq")
    patch = order_ref[lax.axis_index("section")]
    copies = []
    for i in range(patches - 1):
        stale = lax.rem(patch + (i + 1), patches)
        copies.append(pltpu.make_async_copy(cache_ref.at[0, stale], held.at[i], sems.at[i]))
    for copy in copies:
        copy.start()
    for copy in copies:
        copy.wait()
    rows = (patches - 1) * tokens
    for b in range(slots):
        start = pl.multiple_of((mine ^ b) * columns, columns)
        both = held[:, :, :, pl.ds(start, columns)].astype(F32)
        both = both.reshape(rows, 2, columns)
        outs[b][...] = jnp.concatenate([both[:, 0], both[:, 1]], axis=0).astype(BF16)


def project_kernel(step_ref, mod_ref, gain_ref, weight_ref, *refs, slots, tokens, heads, size):
    hidden_refs = refs[:slots][::-1]
    q_ref, held_ref, gate_ref = refs[slots : slots + 3]
    fresh_refs = refs[slots + 3 : 2 * slots + 3]
    mine = lax.axis_index("seq")
    step = step_ref[lax.axis_index("section")]
    columns = heads * size
    shift = mod_ref[0, pl.ds(step, 1), :]
    scale = mod_ref[1, pl.ds(step, 1), :]
    start = pl.multiple_of(mine * columns, columns)
    gate_ref[...] = mod_ref[2, pl.ds(step, 1), pl.ds(start, columns)]
    for b in range(slots):
        held_ref[b] = hidden_refs[b][:, pl.ds(start, columns)]
    rows = jnp.concatenate([r[...].astype(F32) for r in hidden_refs], axis=0)
    normed = (layer_norm(rows) * (1.0 + scale) + shift).astype(BF16)
    parts = []
    for part in range(3):
        dotted = jnp.dot(normed, weight_ref[part], preferred_element_type=F32)
        parts.append(dotted.astype(BF16).astype(F32))
    normed_heads = []
    for part in range(2):
        gain = gain_ref[pl.ds(part, 1), :]
        normed_heads.append(
            jnp.concatenate(
                [head_norm(parts[part][:, h * size : (h + 1) * size], gain) for h in range(heads)], axis=1
            )
        )
    q_ref[...] = normed_heads[0].astype(BF16)
    keys, values = normed_heads[1], parts[2]
    for b in range(slots):
        own = slice(b * tokens, (b + 1) * tokens)
        fresh_refs[b][...] = jnp.concatenate([keys[own], values[own]], axis=0).astype(BF16)


def attend_kernel(q_ref, *refs, slots, tokens, stale, heads, size):
    fresh_refs, old = refs[:slots], refs[slots : 2 * slots][::-1]
    outs = refs[2 * slots : 3 * slots]
    per = stale + tokens
    fresh = [r[...].astype(F32) for r in fresh_refs]
    old = [r[...].astype(F32) for r in old]
    keys = jnp.concatenate([x for b in range(slots) for x in (old[b][:stale], fresh[b][:tokens])], axis=0).astype(BF16)
    values = jnp.concatenate([x for b in range(slots) for x in (old[b][stale:], fresh[b][tokens:])], axis=0).astype(BF16)
    count = slots * per
    queries = q_ref[...]
    length = queries.shape[0]
    lane = lax.broadcasted_iota(jnp.int32, (length, count), 1)
    ones = jnp.ones((count, size), BF16)
    rows = []
    for h in range(heads):
        cut = slice(h * size, (h + 1) * size)
        scores = lax.dot_general(
            queries[:, cut], keys[:, cut], (((1,), (1,)), ((), ())), preferred_element_type=F32
        ) / math.sqrt(size)
        top = jnp.max(scores, axis=-1, keepdims=True)
        weights = jnp.exp(scores - top).astype(BF16).astype(F32)
        apart = jnp.concatenate(
            [jnp.where((lane >= b * per) & (lane < (b + 1) * per), weights, 0.0) for b in range(slots)], axis=0
        ).astype(BF16)
        both = jnp.dot(apart, jnp.concatenate([values[:, cut], ones], axis=1), preferred_element_type=F32)
        both = both.astype(BF16).astype(F32)
        total = both[:length]
        for b in range(1, slots):
            total = total + both[b * length : (b + 1) * length]
        rows.append(total[:, :size] / total[:, size:])
    rows = jnp.concatenate(rows, axis=1)
    pieces = [rows[b * tokens : (b + 1) * tokens] for b in range(slots)]
    for b in range(slots):
        outs[b][:length] = swapped(pieces, b).astype(BF16)
        outs[b][length:] = fresh_refs[b][...]


def output_kernel(gate_ref, held_ref, weight_ref, *refs, slots, tokens):
    columns = weight_ref.shape[1]
    attention = refs[:slots][::-1]
    mine = lax.axis_index("seq")
    total = None
    for b in range(slots):
        start = pl.multiple_of((mine ^ b) * columns, columns)
        term = jnp.dot(attention[b][: slots * tokens], weight_ref[pl.ds(start, columns), :], preferred_element_type=F32)
        total = term if total is None else total + term
    out = total.astype(BF16).astype(F32)
    gate = gate_ref[...]
    for b in range(slots):
        piece = held_ref[b].astype(F32) + gate * out[b * tokens : (b + 1) * tokens]
        refs[slots + b][...] = piece.astype(BF16)


def place_kernel(*refs, slots):
    out_ref, refs = refs[slots], refs[:slots][::-1]
    columns = refs[0].shape[1]
    mine = lax.axis_index("seq")
    for b in range(slots):
        start = pl.multiple_of((mine ^ b) * columns, columns)
        out_ref[0, :, pl.ds(start, columns)] = refs[b][...]


def place_kv_kernel(*refs, slots, tokens):
    out_ref, refs = refs[slots], refs[:slots][::-1]
    columns = refs[0].shape[1]
    mine = lax.axis_index("seq")
    for b in range(slots):
        start = pl.multiple_of((mine ^ b) * columns, columns)
        piece = refs[b][slots * tokens :].astype(F32)
        both = jnp.stack([piece[:tokens], piece[tokens:]], axis=1)
        out_ref[0, :, :, pl.ds(start, columns)] = both.astype(BF16)


def body_by_heads(hidden, kv_cache, w_qkv, w_out, norm_gain, modulation, patch_order, timestep):
    slots, sections = lax.axis_size("seq"), lax.axis_size("section")
    tokens, width = hidden.shape[1:]
    patches = kv_cache.shape[1]
    columns, size = w_qkv.shape[3], norm_gain.shape[2]
    heads, stale = columns // size, (patches - 1) * tokens
    params = pltpu.CompilerParams(vmem_limit_bytes=16 * 2**20)
    shape = jax.ShapeDtypeStruct

    def swap(array, number):
        return lax.ppermute(array, "seq", [(i, i ^ number) for i in range(slots)])

    def swap_all(arrays):
        moved = {b: swap(arrays[b], b) for b in range(slots - 1, 0, -1)}
        return [arrays[0]] + [moved[b] for b in range(1, slots)]

    rows = swap_all([hidden[0]] * slots)
    ahead = pl.pallas_call(
        ahead_kernel,
        out_shape=shape((8, 128), F32),
        out_specs=VMEM,
        compiler_params=params,
        cost_estimate=cost(5e9),
        name="ahead",
    )()
    packed = pl.pallas_call(
        functools.partial(pack_kernel, slots=slots, tokens=tokens, patches=patches, columns=columns),
        out_shape=[shape((2 * stale, columns), BF16)] * slots,
        in_specs=[SMEM, VMEM, HBM],
        out_specs=[VMEM] * slots,
        scratch_shapes=[
            pltpu.VMEM((patches - 1, tokens, 2, width), BF16),
            pltpu.SemaphoreType.DMA((patches - 1,)),
        ],
        compiler_params=params,
        cost_estimate=cost(5e9),
        name="pack",
    )(patch_order, ahead, kv_cache)
    old = swap_all(packed)
    queries, held, gate, *fresh = pl.pallas_call(
        functools.partial(project_kernel, slots=slots, tokens=tokens, heads=heads, size=size),
        out_shape=[
            shape((slots * tokens, columns), BF16),
            shape((slots, tokens, columns), BF16),
            shape((1, columns), F32),
        ]
        + [shape((2 * tokens, columns), BF16)] * slots,
        in_specs=[SMEM] + [VMEM] * (3 + slots),
        out_specs=[VMEM] * (3 + slots),
        compiler_params=params,
        cost_estimate=cost(2e9),
        name="project",
    )(
        timestep,
        jnp.transpose(modulation[0], (1, 0, 2)),
        norm_gain[0],
        jnp.transpose(w_qkv[0], (1, 0, 2)),
        *rows[::-1],
    )
    ordered = pl.pallas_call(
        functools.partial(attend_kernel, slots=slots, tokens=tokens, stale=stale, heads=heads, size=size),
        out_shape=[shape(((slots + 2) * tokens, columns), BF16)] * slots,
        in_specs=[VMEM] * (1 + 2 * slots),
        out_specs=[VMEM] * slots,
        compiler_params=params,
        cost_estimate=cost(2e9),
        name="attend",
    )(queries, *fresh, *old[::-1])
    attention = swap_all(ordered)
    pieces = pl.pallas_call(
        functools.partial(output_kernel, slots=slots, tokens=tokens),
        out_shape=[shape((tokens, columns), BF16)] * slots,
        in_specs=[VMEM] * (3 + slots),
        out_specs=[VMEM] * slots,
        compiler_params=params,
        cost_estimate=cost(2e9),
        name="output",
    )(gate, held, w_out[0], *attention[::-1])

    def onward(array, number):
        pairs = [
            (j * sections + s, (j ^ number) * sections + (s + 1) % sections)
            for j in range(slots)
            for s in range(sections)
        ]
        return lax.ppermute(array, ("seq", "section"), pairs)

    arrived = [onward(pieces[b], b) for b in range(slots - 1, -1, -1)][::-1]
    fresh_kv = pl.pallas_call(
        functools.partial(place_kv_kernel, slots=slots, tokens=tokens),
        out_shape=shape((1, tokens, 2, width), BF16),
        in_specs=[VMEM] * slots,
        out_specs=VMEM,
        compiler_params=params,
        cost_estimate=cost(1e9),
        name="place_kv",
    )(*attention[::-1])
    next_hidden = pl.pallas_call(
        functools.partial(place_kernel, slots=slots),
        out_shape=shape((1, tokens, width), BF16),
        in_specs=[VMEM] * slots,
        out_specs=VMEM,
        compiler_params=params,
        cost_estimate=cost(1e9),
        name="place",
    )(*arrived[::-1])
    return (next_hidden, fresh_kv)


def body_by_tokens(hidden, kv_cache, w_qkv, w_out, norm_gain, modulation, patch_order, timestep):
    section_index = lax.axis_index("section")
    patch_index = lax.dynamic_index_in_dim(patch_order, section_index, 0, keepdims=False)
    step_index = lax.dynamic_index_in_dim(timestep, section_index, 0, keepdims=False)
    modulate = lax.dynamic_index_in_dim(modulation[0], step_index, 0, keepdims=False)
    model_width = hidden.shape[2]
    head_size = norm_gain.shape[2]
    head_count = model_width // head_size
    col_width = w_qkv.shape[3]
    rows_in = hidden[0].astype(jnp.float32)
    own_count = rows_in.shape[0]
    normed = (layer_norm(rows_in) * (1.0 + modulate[1]) + modulate[0]).astype(jnp.bfloat16)
    w_local = w_qkv[0].reshape(model_width, 3 * col_width)
    projected = jnp.dot(
        lax.all_gather(normed, "seq", axis=0, tiled=True),
        w_local,
        preferred_element_type=jnp.float32,
    ).astype(jnp.bfloat16)
    patch_len = projected.shape[0]
    projected = projected.reshape(patch_len, 3, col_width)
    query_cols = lax.all_gather(projected[:, 0], "seq", axis=1, tiled=True)
    kv_rows = lax.all_to_all(projected[:, 1:], "seq", split_axis=0, concat_axis=2, tiled=True)
    queries = head_norm(
        query_cols.astype(jnp.float32).reshape(patch_len, head_count, head_size), norm_gain[0, 0]
    ).astype(jnp.bfloat16)
    key_rows = head_norm(
        kv_rows[:, 0].astype(jnp.float32).reshape(own_count, head_count, head_size), norm_gain[0, 1]
    ).astype(jnp.bfloat16)
    fresh = jnp.stack([key_rows.reshape(own_count, model_width), kv_rows[:, 1]], axis=1)
    zero = jnp.zeros((), jnp.int32)
    local_kv = lax.dynamic_update_slice(kv_cache[0], fresh[None], (patch_index, zero, zero, zero))
    patch_count = local_kv.shape[0]
    local_keys = local_kv[:, :, 0].reshape(patch_count * own_count, head_count, head_size)
    local_values = local_kv[:, :, 1].reshape(patch_count * own_count, head_count, head_size)
    scores = jnp.einsum(
        "thd,shd->hts", queries, local_keys, preferred_element_type=jnp.float32
    ) / math.sqrt(head_size)
    row_top = lax.pmax(jnp.max(scores, axis=-1), "seq")
    weights = jnp.exp(scores - row_top[:, :, None]).astype(jnp.bfloat16)
    denominator = jnp.sum(weights, axis=-1, dtype=jnp.float32).T
    numerator = jnp.einsum(
        "hts,shd->thd", weights, local_values, preferred_element_type=jnp.float32
    ).reshape(patch_len, model_width)
    totals, counts = (
        lax.psum(numerator.astype(jnp.bfloat16), "seq").astype(jnp.float32),
        lax.psum(denominator.astype(jnp.bfloat16), "seq").astype(jnp.float32),
    )
    attention = (totals.reshape(patch_len, head_count, head_size) / counts[:, :, None]).astype(
        jnp.bfloat16
    )
    attention = attention.reshape(patch_len, model_width)
    out_cols = jnp.dot(attention, w_out[0], preferred_element_type=jnp.float32).astype(jnp.bfloat16)
    out_rows = lax.all_to_all(out_cols, "seq", split_axis=0, concat_axis=1, tiled=True)
    block = (rows_in + modulate[2] * out_rows.astype(jnp.float32)).astype(jnp.bfloat16)
    arrived = passed_along(block, "section", 1)
    return (arrived[None], fresh[None])


def body(hidden, kv_cache, w_qkv, w_out, norm_gain, modulation, patch_order, timestep):
    count = lax.axis_size("seq")
    whole_heads = w_qkv.shape[3] % norm_gain.shape[2] == 0
    chosen = body_by_heads if whole_heads and count & (count - 1) == 0 else body_by_tokens
    return chosen(hidden, kv_cache, w_qkv, w_out, norm_gain, modulation, patch_order, timestep)


def solution(mesh):
    return jax.shard_map(
        body,
        mesh=mesh,
        in_specs=(
            P("section", ("groups", "seq"), None),
            P("section", None, ("groups", "seq"), None, None),
            P("section", None, None, "seq"),
            P("section", None, "seq"),
            P("section", None, None),
            P("section", None, None, None),
            P("groups"),
            P("groups"),
        ),
        out_specs=(
            P("section", ("groups", "seq"), None),
            P("section", ("groups", "seq"), None, None),
        ),
        check_vma=False,
    )
```

```python
import functools
import math

import jax
import jax.numpy as jnp
from jax import lax
from jax.experimental import pallas as pl
from jax.experimental.pallas import tpu as pltpu
from jax.sharding import PartitionSpec as P


APART = (1, 2)

F32 = jnp.float32
BF16 = jnp.bfloat16
VMEM = pl.BlockSpec(memory_space=pltpu.VMEM)
SMEM = pl.BlockSpec(memory_space=pltpu.SMEM)


def passed_along(array, axis, by):
    count = lax.axis_size(axis)
    return lax.ppermute(array, axis, [(i, (i + by) % count) for i in range(count)])


def layer_norm(values_in):
    center = values_in - jnp.mean(values_in, axis=-1, keepdims=True)
    spread = jnp.mean(center * center, axis=-1, keepdims=True)
    return center * lax.rsqrt(spread + 1e-06)


def head_norm(values_in, gain):
    square = jnp.mean(values_in * values_in, axis=-1, keepdims=True)
    return values_in * lax.rsqrt(square + 1e-06) * gain


def swapped(slots, number):
    return jnp.concatenate([slots[b ^ number] for b in range(len(slots))], axis=0)


def ahead_kernel(out_ref):
    out_ref[...] = jnp.zeros_like(out_ref)


def pack_kernel(order_ref, _, hidden_ref, cache_ref, *outs, slots, patches, columns, split):
    mine = lax.axis_index("seq")
    patch = order_ref[lax.axis_index("section")]
    hidden = hidden_ref[...].astype(F32)
    hidden = [hidden[:, c * columns : (c + 1) * columns] for c in range(slots)]
    hidden = jnp.concatenate(hidden, axis=0).astype(BF16)
    for b in range(slots):
        start = pl.multiple_of((mine ^ b) * columns, columns)
        both = [
            cache_ref[0, lax.rem(patch + i, patches), :, :, pl.ds(start, columns)].astype(F32)
            for i in range(1, patches)
        ]
        both = jnp.concatenate(both, axis=0)
        both = jnp.concatenate([both[:, 0], both[:, 1]], axis=0).astype(BF16)
        outs[b][: both.shape[0]] = both
        if b and b not in split:
            outs[b][both.shape[0] :] = hidden


def project_kernel(step_ref, mod_ref, gain_ref, weight_ref, *refs, slots, tokens, heads, size, stale):
    hidden_refs = refs[:slots][::-1]
    q_ref, held_ref, gate_ref = refs[slots : slots + 3]
    fresh_refs, scratch = refs[slots + 3 : 2 * slots + 3], refs[2 * slots + 3]
    mine = lax.axis_index("seq")
    step = step_ref[lax.axis_index("section")]
    columns = heads * size
    shift = mod_ref[0, pl.ds(step, 1), :]
    scale = mod_ref[1, pl.ds(step, 1), :]
    start = pl.multiple_of(mine * columns, columns)
    gate_ref[...] = mod_ref[2, pl.ds(step, 1), pl.ds(start, columns)]
    rows = []
    for ref in hidden_refs:
        if ref.shape[0] == tokens:
            rows.append(ref[...].astype(F32))
        else:
            cut = ref[2 * stale :].astype(F32)
            rows.append(jnp.concatenate([cut[c * tokens : (c + 1) * tokens] for c in range(slots)], axis=1))
    rows = jnp.concatenate(rows, axis=0)
    scratch[...] = rows
    normed = (layer_norm(rows) * (1.0 + scale) + shift).astype(BF16)
    parts = []
    for part in range(3):
        dotted = jnp.dot(normed, weight_ref[part], preferred_element_type=F32)
        parts.append(dotted.astype(BF16).astype(F32))
    normed_heads = []
    for part in range(2):
        gain = gain_ref[pl.ds(part, 1), :]
        normed_heads.append(
            jnp.concatenate(
                [head_norm(parts[part][:, h * size : (h + 1) * size], gain) for h in range(heads)], axis=1
            )
        )
    q_ref[...] = normed_heads[0].astype(BF16)
    keys, values = normed_heads[1], parts[2]
    for b in range(slots):
        own = slice(b * tokens, (b + 1) * tokens)
        fresh_refs[b][...] = jnp.concatenate([keys[own], values[own]], axis=0).astype(BF16)
    held_ref[...] = scratch[:, pl.ds(start, columns)].astype(BF16)


def attend_kernel(q_ref, *refs, slots, tokens, stale, heads, size):
    fresh_refs, old = refs[:slots], refs[slots : 2 * slots][::-1]
    outs = refs[2 * slots : 3 * slots]
    per = stale + tokens
    fresh = [r[...].astype(F32) for r in fresh_refs]
    old = [r[: 2 * stale].astype(F32) for r in old]
    keys = jnp.concatenate([x for b in range(slots) for x in (old[b][:stale], fresh[b][:tokens])], axis=0).astype(BF16)
    values = jnp.concatenate([x for b in range(slots) for x in (old[b][stale:], fresh[b][tokens:])], axis=0).astype(BF16)
    count = slots * per
    queries = q_ref[...]
    length = queries.shape[0]
    cuts = [slice(h * size, (h + 1) * size) for h in range(heads)]
    dims = (((1,), (1,)), ((), ()))
    scores = [lax.dot_general(queries[:, cut], keys[:, cut], dims, preferred_element_type=F32) for cut in cuts]
    scores = jnp.concatenate(scores, axis=0) / math.sqrt(size)
    top = jnp.max(scores, axis=-1, keepdims=True)
    weights = jnp.exp(scores - top).astype(BF16).astype(F32)
    lane = lax.broadcasted_iota(jnp.int32, weights.shape, 1)
    apart = [jnp.where((lane >= b * per) & (lane < (b + 1) * per), weights, 0.0).astype(BF16) for b in range(slots)]
    ones = jnp.ones((count, size), BF16)
    sums = []
    for h, cut in enumerate(cuts):
        rows = jnp.concatenate([x[h * length : (h + 1) * length] for x in apart], axis=0)
        extended = jnp.concatenate([values[:, cut], ones], axis=1)
        sums.append(jnp.dot(rows, extended, preferred_element_type=F32))
    rows = []
    for both in sums:
        both = both.astype(BF16).astype(F32)
        total = both[:length]
        for b in range(1, slots):
            total = total + both[b * length : (b + 1) * length]
        rows.append(total[:, :size] / total[:, size:])
    rows = jnp.concatenate(rows, axis=1)
    pieces = [rows[b * tokens : (b + 1) * tokens] for b in range(slots)]
    for b in range(slots):
        outs[b][:length] = swapped(pieces, b).astype(BF16)
        outs[b][length:] = fresh_refs[b][...]


def output_kernel(gate_ref, held_ref, weight_ref, *refs, slots, tokens):
    columns = weight_ref.shape[1]
    attention = refs[:slots][::-1]
    mine = lax.axis_index("seq")
    total = None
    for b in range(slots):
        start = pl.multiple_of((mine ^ b) * columns, columns)
        term = jnp.dot(attention[b][: slots * tokens], weight_ref[pl.ds(start, columns), :], preferred_element_type=F32)
        total = term if total is None else total + term
    block = held_ref[...].astype(F32) + gate_ref[...] * total.astype(BF16).astype(F32)
    for b in range(slots):
        refs[slots + b][...] = block[b * tokens : (b + 1) * tokens].astype(BF16)


def place_kernel(*refs, slots):
    out_ref, refs = refs[slots], refs[:slots][::-1]
    columns = refs[0].shape[1]
    mine = lax.axis_index("seq")
    for b in range(slots):
        start = pl.multiple_of((mine ^ b) * columns, columns)
        out_ref[0, :, pl.ds(start, columns)] = refs[b][...]


def place_kv_kernel(*refs, slots, tokens):
    out_ref, refs = refs[slots], refs[:slots][::-1]
    columns = refs[0].shape[1]
    mine = lax.axis_index("seq")
    for b in range(slots):
        start = pl.multiple_of((mine ^ b) * columns, columns)
        piece = refs[b][slots * tokens :].astype(F32)
        both = jnp.stack([piece[:tokens], piece[tokens:]], axis=1)
        out_ref[0, :, :, pl.ds(start, columns)] = both.astype(BF16)


def call(kernel, flops, out_shape, specs, operands, scratch=(), **sizes):
    return pl.pallas_call(
        functools.partial(kernel, **sizes),
        out_shape=out_shape,
        in_specs=specs + [VMEM] * (len(operands) - len(specs)),
        out_specs=jax.tree.map(lambda _: VMEM, out_shape),
        scratch_shapes=scratch,
        compiler_params=pltpu.CompilerParams(vmem_limit_bytes=16 * 2**20),
        cost_estimate=pl.CostEstimate(flops=int(flops), transcendentals=0, bytes_accessed=2**20),
    )(*operands)


def apart(slots):
    return APART if slots > 2 else ()


def body_by_heads(hidden, kv_cache, w_qkv, w_out, norm_gain, modulation, patch_order, timestep):
    slots, sections = lax.axis_size("seq"), lax.axis_size("section")
    tokens, width = hidden.shape[1:]
    patches = kv_cache.shape[1]
    columns, size = w_qkv.shape[3], norm_gain.shape[2]
    heads, stale, rows = columns // size, (patches - 1) * tokens, slots * tokens
    split = apart(slots)

    def array(*shape, dtype=BF16):
        return jax.ShapeDtypeStruct(shape, dtype)

    def moved(array, number, onward=0):
        pairs = [
            (j * sections + s, (j ^ number) * sections + (s + onward) % sections)
            for j in range(slots)
            for s in range(sections)
        ]
        return lax.ppermute(array, ("seq", "section"), pairs)

    def exchanged(arrays):
        return [arrays[0]] + [moved(arrays[b], b) for b in range(1, slots)]

    own = hidden[0]
    alone = {b: moved(own, b) for b in split}
    ahead = call(ahead_kernel, 5e9, array(8, 128, dtype=F32), [], [])
    packed = call(
        pack_kernel,
        5e9,
        [array(2 * stale + (rows if b and b not in split else 0), columns) for b in range(slots)],
        [SMEM],
        [patch_order, ahead, own, kv_cache],
        slots=slots,
        patches=patches,
        columns=columns,
        split=split,
    )
    old = exchanged(packed)
    inputs = [own] + [alone[b] if b in split else old[b] for b in range(1, slots)]
    queries, held, gate, *fresh = call(
        project_kernel,
        2e9,
        [array(rows, columns), array(rows, columns), array(1, columns, dtype=F32)] + [array(2 * tokens, columns)] * slots,
        [SMEM],
        [
            timestep,
            jnp.transpose(modulation[0], (1, 0, 2)),
            norm_gain[0],
            jnp.transpose(w_qkv[0], (1, 0, 2)),
            *inputs[::-1],
        ],
        scratch=[pltpu.VMEM((rows, width), F32)],
        slots=slots,
        tokens=tokens,
        heads=heads,
        size=size,
        stale=stale,
    )
    ordered = call(
        attend_kernel,
        2e9,
        [array(rows + 2 * tokens, columns)] * slots,
        [],
        [queries, *fresh, *old[::-1]],
        slots=slots,
        tokens=tokens,
        stale=stale,
        heads=heads,
        size=size,
    )
    attention = exchanged(ordered)
    pieces = call(
        output_kernel,
        2e9,
        [array(tokens, columns)] * slots,
        [],
        [gate, held, w_out[0], *attention[::-1]],
        slots=slots,
        tokens=tokens,
    )
    arrived = [moved(pieces[b], b, onward=1) for b in range(slots)]
    fresh_kv = call(place_kv_kernel, 1e9, array(1, tokens, 2, width), [], attention[::-1], slots=slots, tokens=tokens)
    next_hidden = call(place_kernel, 1e9, array(1, tokens, width), [], arrived[::-1], slots=slots)
    return (next_hidden, fresh_kv)


def body_by_tokens(hidden, kv_cache, w_qkv, w_out, norm_gain, modulation, patch_order, timestep):
    section_index = lax.axis_index("section")
    patch_index = lax.dynamic_index_in_dim(patch_order, section_index, 0, keepdims=False)
    step_index = lax.dynamic_index_in_dim(timestep, section_index, 0, keepdims=False)
    modulate = lax.dynamic_index_in_dim(modulation[0], step_index, 0, keepdims=False)
    model_width = hidden.shape[2]
    head_size = norm_gain.shape[2]
    head_count = model_width // head_size
    col_width = w_qkv.shape[3]
    rows_in = hidden[0].astype(jnp.float32)
    own_count = rows_in.shape[0]
    normed = (layer_norm(rows_in) * (1.0 + modulate[1]) + modulate[0]).astype(jnp.bfloat16)
    w_local = w_qkv[0].reshape(model_width, 3 * col_width)
    projected = jnp.dot(
        lax.all_gather(normed, "seq", axis=0, tiled=True),
        w_local,
        preferred_element_type=jnp.float32,
    ).astype(jnp.bfloat16)
    patch_len = projected.shape[0]
    projected = projected.reshape(patch_len, 3, col_width)
    query_cols = lax.all_gather(projected[:, 0], "seq", axis=1, tiled=True)
    kv_rows = lax.all_to_all(projected[:, 1:], "seq", split_axis=0, concat_axis=2, tiled=True)
    queries = head_norm(
        query_cols.astype(jnp.float32).reshape(patch_len, head_count, head_size), norm_gain[0, 0]
    ).astype(jnp.bfloat16)
    key_rows = head_norm(
        kv_rows[:, 0].astype(jnp.float32).reshape(own_count, head_count, head_size), norm_gain[0, 1]
    ).astype(jnp.bfloat16)
    fresh = jnp.stack([key_rows.reshape(own_count, model_width), kv_rows[:, 1]], axis=1)
    zero = jnp.zeros((), jnp.int32)
    local_kv = lax.dynamic_update_slice(kv_cache[0], fresh[None], (patch_index, zero, zero, zero))
    patch_count = local_kv.shape[0]
    local_keys = local_kv[:, :, 0].reshape(patch_count * own_count, head_count, head_size)
    local_values = local_kv[:, :, 1].reshape(patch_count * own_count, head_count, head_size)
    scores = jnp.einsum(
        "thd,shd->hts", queries, local_keys, preferred_element_type=jnp.float32
    ) / math.sqrt(head_size)
    row_top = lax.pmax(jnp.max(scores, axis=-1), "seq")
    weights = jnp.exp(scores - row_top[:, :, None]).astype(jnp.bfloat16)
    denominator = jnp.sum(weights, axis=-1, dtype=jnp.float32).T
    numerator = jnp.einsum(
        "hts,shd->thd", weights, local_values, preferred_element_type=jnp.float32
    ).reshape(patch_len, model_width)
    totals, counts = (
        lax.psum(numerator.astype(jnp.bfloat16), "seq").astype(jnp.float32),
        lax.psum(denominator.astype(jnp.bfloat16), "seq").astype(jnp.float32),
    )
    attention = (totals.reshape(patch_len, head_count, head_size) / counts[:, :, None]).astype(
        jnp.bfloat16
    )
    attention = attention.reshape(patch_len, model_width)
    out_cols = jnp.dot(attention, w_out[0], preferred_element_type=jnp.float32).astype(jnp.bfloat16)
    out_rows = lax.all_to_all(out_cols, "seq", split_axis=0, concat_axis=1, tiled=True)
    block = (rows_in + modulate[2] * out_rows.astype(jnp.float32)).astype(jnp.bfloat16)
    arrived = passed_along(block, "section", 1)
    return (arrived[None], fresh[None])


def body(hidden, kv_cache, w_qkv, w_out, norm_gain, modulation, patch_order, timestep):
    count = lax.axis_size("seq")
    whole_heads = w_qkv.shape[3] % norm_gain.shape[2] == 0
    chosen = body_by_heads if whole_heads and count & (count - 1) == 0 else body_by_tokens
    return chosen(hidden, kv_cache, w_qkv, w_out, norm_gain, modulation, patch_order, timestep)


def solution(mesh):
    return jax.shard_map(
        body,
        mesh=mesh,
        in_specs=(
            P("section", ("groups", "seq"), None),
            P("section", None, ("groups", "seq"), None, None),
            P("section", None, None, "seq"),
            P("section", None, "seq"),
            P("section", None, None),
            P("section", None, None, None),
            P("groups"),
            P("groups"),
        ),
        out_specs=(
            P("section", ("groups", "seq"), None),
            P("section", ("groups", "seq"), None, None),
        ),
        check_vma=False,
    )
```

```python
import functools
import math

import jax
import jax.numpy as jnp
from jax import lax
from jax.experimental import pallas as pl
from jax.experimental.pallas import tpu as pltpu
from jax.sharding import PartitionSpec as P


APART = (1, 2)
TURNS = ((3, 2), (0, 3), (2, 1), (1, 0))

F32 = jnp.float32
BF16 = jnp.bfloat16
VMEM = pl.BlockSpec(memory_space=pltpu.VMEM)
SMEM = pl.BlockSpec(memory_space=pltpu.SMEM)


def passed_along(array, axis, by):
    count = lax.axis_size(axis)
    return lax.ppermute(array, axis, [(i, (i + by) % count) for i in range(count)])


def layer_norm(values_in):
    center = values_in - jnp.mean(values_in, axis=-1, keepdims=True)
    spread = jnp.mean(center * center, axis=-1, keepdims=True)
    return center * lax.rsqrt(spread + 1e-06)


def head_norm(values_in, gain):
    square = jnp.mean(values_in * values_in, axis=-1, keepdims=True)
    return values_in * lax.rsqrt(square + 1e-06) * gain


def swapped(slots, number):
    return jnp.concatenate([slots[b ^ number] for b in range(len(slots))], axis=0)


def ahead_kernel(out_ref):
    out_ref[...] = jnp.zeros_like(out_ref)


def pack_kernel(order_ref, _, hidden_ref, cache_ref, *outs, slots, patches, columns, split):
    mine = lax.axis_index("seq")
    patch = order_ref[lax.axis_index("section")]
    hidden = hidden_ref[...].astype(F32)
    hidden = [hidden[:, c * columns : (c + 1) * columns] for c in range(slots)]
    hidden = jnp.concatenate(hidden, axis=0).astype(BF16)
    for b in range(slots):
        start = pl.multiple_of((mine ^ b) * columns, columns)
        both = [
            cache_ref[0, lax.rem(patch + i, patches), :, :, pl.ds(start, columns)].astype(F32)
            for i in range(1, patches)
        ]
        both = jnp.concatenate(both, axis=0)
        both = jnp.concatenate([both[:, 0], both[:, 1]], axis=0).astype(BF16)
        outs[b][: both.shape[0]] = both
        if b and b not in split:
            outs[b][both.shape[0] :] = hidden


def project_kernel(step_ref, mod_ref, gain_ref, weight_ref, *refs, slots, tokens, heads, size, stale):
    hidden_refs = refs[:slots][::-1]
    q_ref, held_ref, gate_ref = refs[slots : slots + 3]
    fresh_refs, scratch = refs[slots + 3 : 2 * slots + 3], refs[2 * slots + 3]
    mine = lax.axis_index("seq")
    step = step_ref[lax.axis_index("section")]
    columns = heads * size
    shift = mod_ref[0, pl.ds(step, 1), :]
    scale = mod_ref[1, pl.ds(step, 1), :]
    start = pl.multiple_of(mine * columns, columns)
    gate_ref[...] = mod_ref[2, pl.ds(step, 1), pl.ds(start, columns)]
    rows = []
    for ref in hidden_refs:
        if ref.shape[0] == tokens:
            rows.append(ref[...].astype(F32))
        else:
            cut = ref[2 * stale :].astype(F32)
            rows.append(jnp.concatenate([cut[c * tokens : (c + 1) * tokens] for c in range(slots)], axis=1))
    rows = jnp.concatenate(rows, axis=0)
    scratch[...] = rows
    normed = (layer_norm(rows) * (1.0 + scale) + shift).astype(BF16)
    parts = []
    for part in range(3):
        dotted = jnp.dot(normed, weight_ref[part], preferred_element_type=F32)
        parts.append(dotted.astype(BF16).astype(F32))
    normed_heads = []
    for part in range(2):
        stacked = jnp.concatenate([parts[part][:, h * size : (h + 1) * size] for h in range(heads)], axis=0)
        stacked = head_norm(stacked, gain_ref[pl.ds(part, 1), :])
        length = slots * tokens
        normed_heads.append(
            jnp.concatenate([stacked[h * length : (h + 1) * length] for h in range(heads)], axis=1)
        )
    q_ref[...] = normed_heads[0].astype(BF16)
    keys, values = normed_heads[1], parts[2]
    for b in range(slots):
        own = slice(b * tokens, (b + 1) * tokens)
        fresh_refs[b][...] = jnp.concatenate([keys[own], values[own]], axis=0).astype(BF16)
    held_ref[...] = scratch[:, pl.ds(start, columns)].astype(BF16)


def attend_kernel(q_ref, *refs, slots, tokens, stale, heads, size):
    fresh_refs, old = refs[:slots], refs[slots : 2 * slots][::-1]
    outs = refs[2 * slots : 3 * slots]
    per = stale + tokens
    fresh = [r[...].astype(F32) for r in fresh_refs]
    old = [r[: 2 * stale].astype(F32) for r in old]
    keys = jnp.concatenate([x for b in range(slots) for x in (old[b][:stale], fresh[b][:tokens])], axis=0).astype(BF16)
    values = jnp.concatenate([x for b in range(slots) for x in (old[b][stale:], fresh[b][tokens:])], axis=0).astype(BF16)
    count = slots * per
    queries = q_ref[...]
    length = queries.shape[0]
    cuts = [slice(h * size, (h + 1) * size) for h in range(heads)]
    dims = (((1,), (1,)), ((), ()))
    scores = [lax.dot_general(queries[:, cut], keys[:, cut], dims, preferred_element_type=F32) for cut in cuts]
    scores = jnp.concatenate(scores, axis=0) / math.sqrt(size)
    top = jnp.max(scores, axis=-1, keepdims=True)
    weights = jnp.exp(scores - top).astype(BF16).astype(F32)
    lane = lax.broadcasted_iota(jnp.int32, weights.shape, 1)
    apart = [jnp.where((lane >= b * per) & (lane < (b + 1) * per), weights, 0.0).astype(BF16) for b in range(slots)]
    ones = jnp.ones((count, size), BF16)
    sums = []
    for h, cut in enumerate(cuts):
        rows = jnp.concatenate([x[h * length : (h + 1) * length] for x in apart], axis=0)
        extended = jnp.concatenate([values[:, cut], ones], axis=1)
        sums.append(jnp.dot(rows, extended, preferred_element_type=F32))
    rows = []
    for both in sums:
        both = both.astype(BF16).astype(F32)
        total = both[:length]
        for b in range(1, slots):
            total = total + both[b * length : (b + 1) * length]
        rows.append(total[:, :size] / total[:, size:])
    rows = jnp.concatenate(rows, axis=1)
    pieces = [rows[b * tokens : (b + 1) * tokens] for b in range(slots)]
    for b in range(slots):
        outs[b][:length] = swapped(pieces, b).astype(BF16)
        outs[b][length:] = fresh_refs[b][...]


def partial_kernel(weight_ref, *refs, numbers, rows, before):
    columns = weight_ref.shape[1]
    mine = lax.axis_index("seq")
    total = refs[len(numbers)][...] if before else None
    for ref, b in zip(refs[: len(numbers)], numbers, strict=True):
        start = pl.multiple_of((mine ^ b) * columns, columns)
        term = jnp.dot(ref[:rows], weight_ref[pl.ds(start, columns), :], preferred_element_type=F32)
        total = term if total is None else total + term
    refs[-1][...] = total


def output_kernel(gate_ref, held_ref, weight_ref, total_ref, attention_ref, *outs, number, tokens, turns):
    columns = weight_ref.shape[1]
    start = pl.multiple_of((lax.axis_index("seq") ^ number) * columns, columns)
    rows = total_ref.shape[0]
    total = total_ref[...] + jnp.dot(
        attention_ref[:rows], weight_ref[pl.ds(start, columns), :], preferred_element_type=F32
    )
    block = held_ref[...].astype(F32) + gate_ref[...] * total.astype(BF16).astype(F32)
    pieces = [block[b * tokens : (b + 1) * tokens] for b in range(len(outs))]
    even = lax.rem(lax.axis_index("section"), 2) == 0
    for out, (b, c) in zip(outs, turns, strict=True):
        out[...] = jnp.where(even, pieces[b], pieces[c]).astype(BF16)


def place_kernel(*refs, slots, turns):
    out_ref, refs = refs[slots], refs[:slots][::-1]
    columns = refs[0].shape[1]
    mine, sections = lax.axis_index("seq"), lax.axis_size("section")
    even = lax.rem(lax.axis_index("section") + (sections - 1), sections) % 2 == 0
    for ref, (b, c) in zip(refs, turns, strict=True):
        start = pl.multiple_of((mine ^ jnp.where(even, b, c)) * columns, columns)
        out_ref[0, :, pl.ds(start, columns)] = ref[...]


def place_kv_kernel(*refs, slots, tokens):
    out_ref, refs = refs[slots], refs[:slots][::-1]
    columns = refs[0].shape[1]
    mine = lax.axis_index("seq")
    for b in range(slots):
        start = pl.multiple_of((mine ^ b) * columns, columns)
        piece = refs[b][slots * tokens :].astype(F32)
        both = jnp.stack([piece[:tokens], piece[tokens:]], axis=1)
        out_ref[0, :, :, pl.ds(start, columns)] = both.astype(BF16)


def call(kernel, flops, out_shape, specs, operands, scratch=(), **sizes):
    return pl.pallas_call(
        functools.partial(kernel, **sizes),
        out_shape=out_shape,
        in_specs=specs + [VMEM] * (len(operands) - len(specs)),
        out_specs=jax.tree.map(lambda _: VMEM, out_shape),
        scratch_shapes=scratch,
        compiler_params=pltpu.CompilerParams(vmem_limit_bytes=16 * 2**20),
        cost_estimate=pl.CostEstimate(flops=int(flops), transcendentals=0, bytes_accessed=2**20),
    )(*operands)


def apart(slots):
    return APART if slots > 2 else ()


def body_by_heads(hidden, kv_cache, w_qkv, w_out, norm_gain, modulation, patch_order, timestep):
    slots, sections = lax.axis_size("seq"), lax.axis_size("section")
    tokens, width = hidden.shape[1:]
    patches = kv_cache.shape[1]
    columns, size = w_qkv.shape[3], norm_gain.shape[2]
    heads, stale, rows = columns // size, (patches - 1) * tokens, slots * tokens
    split = apart(slots)
    turns = TURNS if slots == 4 else [(b, b) for b in range(slots)]

    def array(*shape, dtype=BF16):
        return jax.ShapeDtypeStruct(shape, dtype)

    def moved(array, number):
        return lax.ppermute(array, "seq", [(j, j ^ number) for j in range(slots)])

    def onward(array, turn):
        pairs = [
            (j * sections + s, (j ^ turn[s % 2]) * sections + (s + 1) % sections)
            for j in range(slots)
            for s in range(sections)
        ]
        return lax.ppermute(array, ("seq", "section"), pairs)

    def exchanged(arrays):
        return [arrays[0]] + [moved(arrays[b], b) for b in range(1, slots)]

    own = hidden[0]
    alone = {b: moved(own, b) for b in split}
    ahead = call(ahead_kernel, 5e9, array(8, 128, dtype=F32), [], [])
    packed = call(
        pack_kernel,
        5e9,
        [array(2 * stale + (rows if b and b not in split else 0), columns) for b in range(slots)],
        [SMEM],
        [patch_order, ahead, own, kv_cache],
        slots=slots,
        patches=patches,
        columns=columns,
        split=split,
    )
    old = exchanged(packed)
    inputs = [own] + [alone[b] if b in split else old[b] for b in range(1, slots)]
    queries, held, gate, *fresh = call(
        project_kernel,
        2e9,
        [array(rows, columns), array(rows, columns), array(1, columns, dtype=F32)] + [array(2 * tokens, columns)] * slots,
        [SMEM],
        [
            timestep,
            jnp.transpose(modulation[0], (1, 0, 2)),
            norm_gain[0],
            jnp.transpose(w_qkv[0], (1, 0, 2)),
            *inputs[::-1],
        ],
        scratch=[pltpu.VMEM((rows, width), F32)],
        slots=slots,
        tokens=tokens,
        heads=heads,
        size=size,
        stale=stale,
    )
    ordered = call(
        attend_kernel,
        2e9,
        [array(rows + 2 * tokens, columns)] * slots,
        [],
        [queries, *fresh, *old[::-1]],
        slots=slots,
        tokens=tokens,
        stale=stale,
        heads=heads,
        size=size,
    )
    attention = exchanged(ordered)
    weights = w_out[0]
    groups = [(0, slots - 1)] + [(b,) for b in range(slots - 2, 1, -1)] if slots > 2 else [(0,)]
    total = []
    for numbers in groups:
        operands = [weights] + [attention[b] for b in numbers] + total
        total = [
            call(
                partial_kernel,
                1e9,
                array(rows, columns, dtype=F32),
                [],
                operands,
                numbers=numbers,
                rows=rows,
                before=bool(total),
            )
        ]
    pieces = call(
        output_kernel,
        2e9,
        [array(tokens, columns)] * slots,
        [],
        [gate, held, weights, *total, attention[1]],
        number=1,
        tokens=tokens,
        turns=turns,
    )
    arrived = [onward(piece, turn) for piece, turn in zip(pieces, turns, strict=True)]
    fresh_kv = call(place_kv_kernel, 1e9, array(1, tokens, 2, width), [], attention[::-1], slots=slots, tokens=tokens)
    next_hidden = call(place_kernel, 1e9, array(1, tokens, width), [], arrived[::-1], slots=slots, turns=turns)
    return (next_hidden, fresh_kv)


def body_by_tokens(hidden, kv_cache, w_qkv, w_out, norm_gain, modulation, patch_order, timestep):
    section_index = lax.axis_index("section")
    patch_index = lax.dynamic_index_in_dim(patch_order, section_index, 0, keepdims=False)
    step_index = lax.dynamic_index_in_dim(timestep, section_index, 0, keepdims=False)
    modulate = lax.dynamic_index_in_dim(modulation[0], step_index, 0, keepdims=False)
    model_width = hidden.shape[2]
    head_size = norm_gain.shape[2]
    head_count = model_width // head_size
    col_width = w_qkv.shape[3]
    rows_in = hidden[0].astype(jnp.float32)
    own_count = rows_in.shape[0]
    normed = (layer_norm(rows_in) * (1.0 + modulate[1]) + modulate[0]).astype(jnp.bfloat16)
    w_local = w_qkv[0].reshape(model_width, 3 * col_width)
    projected = jnp.dot(
        lax.all_gather(normed, "seq", axis=0, tiled=True),
        w_local,
        preferred_element_type=jnp.float32,
    ).astype(jnp.bfloat16)
    patch_len = projected.shape[0]
    projected = projected.reshape(patch_len, 3, col_width)
    query_cols = lax.all_gather(projected[:, 0], "seq", axis=1, tiled=True)
    kv_rows = lax.all_to_all(projected[:, 1:], "seq", split_axis=0, concat_axis=2, tiled=True)
    queries = head_norm(
        query_cols.astype(jnp.float32).reshape(patch_len, head_count, head_size), norm_gain[0, 0]
    ).astype(jnp.bfloat16)
    key_rows = head_norm(
        kv_rows[:, 0].astype(jnp.float32).reshape(own_count, head_count, head_size), norm_gain[0, 1]
    ).astype(jnp.bfloat16)
    fresh = jnp.stack([key_rows.reshape(own_count, model_width), kv_rows[:, 1]], axis=1)
    zero = jnp.zeros((), jnp.int32)
    local_kv = lax.dynamic_update_slice(kv_cache[0], fresh[None], (patch_index, zero, zero, zero))
    patch_count = local_kv.shape[0]
    local_keys = local_kv[:, :, 0].reshape(patch_count * own_count, head_count, head_size)
    local_values = local_kv[:, :, 1].reshape(patch_count * own_count, head_count, head_size)
    scores = jnp.einsum(
        "thd,shd->hts", queries, local_keys, preferred_element_type=jnp.float32
    ) / math.sqrt(head_size)
    row_top = lax.pmax(jnp.max(scores, axis=-1), "seq")
    weights = jnp.exp(scores - row_top[:, :, None]).astype(jnp.bfloat16)
    denominator = jnp.sum(weights, axis=-1, dtype=jnp.float32).T
    numerator = jnp.einsum(
        "hts,shd->thd", weights, local_values, preferred_element_type=jnp.float32
    ).reshape(patch_len, model_width)
    totals, counts = (
        lax.psum(numerator.astype(jnp.bfloat16), "seq").astype(jnp.float32),
        lax.psum(denominator.astype(jnp.bfloat16), "seq").astype(jnp.float32),
    )
    attention = (totals.reshape(patch_len, head_count, head_size) / counts[:, :, None]).astype(
        jnp.bfloat16
    )
    attention = attention.reshape(patch_len, model_width)
    out_cols = jnp.dot(attention, w_out[0], preferred_element_type=jnp.float32).astype(jnp.bfloat16)
    out_rows = lax.all_to_all(out_cols, "seq", split_axis=0, concat_axis=1, tiled=True)
    block = (rows_in + modulate[2] * out_rows.astype(jnp.float32)).astype(jnp.bfloat16)
    arrived = passed_along(block, "section", 1)
    return (arrived[None], fresh[None])


def body(hidden, kv_cache, w_qkv, w_out, norm_gain, modulation, patch_order, timestep):
    count = lax.axis_size("seq")
    whole_heads = w_qkv.shape[3] % norm_gain.shape[2] == 0
    chosen = body_by_heads if whole_heads and count & (count - 1) == 0 else body_by_tokens
    return chosen(hidden, kv_cache, w_qkv, w_out, norm_gain, modulation, patch_order, timestep)


def solution(mesh):
    return jax.shard_map(
        body,
        mesh=mesh,
        in_specs=(
            P("section", ("groups", "seq"), None),
            P("section", None, ("groups", "seq"), None, None),
            P("section", None, None, "seq"),
            P("section", None, "seq"),
            P("section", None, None),
            P("section", None, None, None),
            P("groups"),
            P("groups"),
        ),
        out_specs=(
            P("section", ("groups", "seq"), None),
            P("section", ("groups", "seq"), None, None),
        ),
        check_vma=False,
    )
```

```python
import functools
import math

import jax
import jax.numpy as jnp
from jax import lax
from jax.experimental import pallas as pl
from jax.experimental.pallas import tpu as pltpu
from jax.sharding import PartitionSpec as P


APART = (1, 2)
TURNS = ((3, 2), (0, 3), (2, 1), (1, 0))

F32 = jnp.float32
BF16 = jnp.bfloat16
VMEM = pl.BlockSpec(memory_space=pltpu.VMEM)


def passed_along(array, axis, by):
    count = lax.axis_size(axis)
    return lax.ppermute(array, axis, [(i, (i + by) % count) for i in range(count)])


def layer_norm(values_in):
    center = values_in - jnp.mean(values_in, axis=-1, keepdims=True)
    spread = jnp.mean(center * center, axis=-1, keepdims=True)
    return center * lax.rsqrt(spread + 1e-06)


def head_norm(values_in, gain):
    square = jnp.mean(values_in * values_in, axis=-1, keepdims=True)
    return values_in * lax.rsqrt(square + 1e-06) * gain


def swapped(slots, number):
    return jnp.concatenate([slots[b ^ number] for b in range(len(slots))], axis=0)


def ahead_kernel(out_ref):
    out_ref[...] = jnp.zeros_like(out_ref)


def entry(ref):
    lane = lax.broadcasted_iota(jnp.int32, ref.shape, 1)
    mine = lane == lax.axis_index("section")
    return jnp.sum(jnp.where(mine, ref[...], 0).astype(F32), axis=1, keepdims=True)


def pack_kernel(order_ref, _, hidden_ref, cache_ref, *outs, numbers, slots, patches, columns, split):
    mine = lax.axis_index("seq")
    patch = entry(order_ref)
    for out, b in zip(outs, numbers, strict=True):
        start = pl.multiple_of((mine ^ b) * columns, columns)
        both = [cache_ref[0, p, :, :, pl.ds(start, columns)].astype(F32) for p in range(patches)]
        both = [x[:, part] for part in range(2) for x in both]
        stale = []
        for part in range(2):
            for i in range(part * patches, (part + 1) * patches - 1):
                stale.append(jnp.where(patch > i - part * patches, both[i], both[i + 1]))
        stale = jnp.concatenate(stale, axis=0).astype(BF16)
        out[: stale.shape[0]] = stale
        if b and b not in split:
            hidden = hidden_ref[...].astype(F32)
            hidden = [hidden[:, c * columns : (c + 1) * columns] for c in range(slots)]
            out[stale.shape[0] :] = jnp.concatenate(hidden, axis=0).astype(BF16)


def project_kernel(step_ref, mod_ref, gain_ref, weight_ref, *refs, slots, tokens, heads, size, stale):
    hidden_refs = refs[:slots][::-1]
    q_ref, k_ref, normed_ref, held_ref, gate_ref, scratch = refs[slots:]
    mine = lax.axis_index("seq")
    columns, length = heads * size, slots * tokens
    step = lax.broadcasted_iota(jnp.int32, (mod_ref.shape[1], 1), 0).astype(F32) == entry(step_ref)
    modulate = [jnp.sum(jnp.where(step, mod_ref[i], 0.0), axis=0, keepdims=True) for i in range(2)]
    start = pl.multiple_of(mine * columns, columns)
    rows = []
    for ref in hidden_refs:
        if ref.shape[0] == tokens:
            rows.append(ref[...].astype(F32))
        else:
            cut = ref[2 * stale :].astype(F32)
            rows.append(jnp.concatenate([cut[c * tokens : (c + 1) * tokens] for c in range(slots)], axis=1))
    rows = jnp.concatenate(rows, axis=0)
    normed = (layer_norm(rows) * (1.0 + modulate[1]) + modulate[0]).astype(BF16)
    normed_ref[...] = normed
    for part, out in enumerate((q_ref, k_ref)):
        dotted = jnp.dot(normed, weight_ref[part], preferred_element_type=F32).astype(BF16).astype(F32)
        stacked = jnp.concatenate([dotted[:, h * size : (h + 1) * size] for h in range(heads)], axis=0)
        stacked = head_norm(stacked, gain_ref[pl.ds(part, 1), :]).astype(BF16)
        for h in range(heads):
            out[:, h * size : (h + 1) * size] = stacked[h * length : (h + 1) * length]
    scratch[...] = rows
    held_ref[...] = scratch[:, pl.ds(start, columns)].astype(BF16)
    gates = jnp.where(step, mod_ref[2, :, pl.ds(start, columns)], 0.0)
    gate_ref[...] = jnp.sum(gates, axis=0, keepdims=True)


def attend_kernel(q_ref, k_ref, normed_ref, weight_ref, *refs, slots, tokens, stale, heads, size):
    old, outs = refs[:slots][::-1], refs[slots:]
    old = [r[: 2 * stale].astype(F32) for r in old]
    fresh_keys = k_ref[...].astype(F32)
    own = [slice(b * tokens, (b + 1) * tokens) for b in range(slots)]
    per = stale + tokens
    count = slots * per
    keys = jnp.concatenate([x for b in range(slots) for x in (old[b][:stale], fresh_keys[own[b]])], axis=0).astype(BF16)
    queries = q_ref[...]
    length = queries.shape[0]
    cuts = [slice(h * size, (h + 1) * size) for h in range(heads)]
    dims = (((1,), (1,)), ((), ()))
    scores = [lax.dot_general(queries[:, cut], keys[:, cut], dims, preferred_element_type=F32) for cut in cuts]
    fresh_values = jnp.dot(normed_ref[...], weight_ref[2], preferred_element_type=F32).astype(BF16).astype(F32)
    scores = jnp.concatenate(scores, axis=0) / math.sqrt(size)
    top = jnp.max(scores, axis=-1, keepdims=True)
    weights = jnp.exp(scores - top).astype(BF16).astype(F32)
    values = [x for b in range(slots) for x in (old[b][stale:], fresh_values[own[b]])]
    values = jnp.concatenate(values, axis=0).astype(BF16)
    lane = lax.broadcasted_iota(jnp.int32, weights.shape, 1)
    apart = [jnp.where((lane >= b * per) & (lane < (b + 1) * per), weights, 0.0).astype(BF16) for b in range(slots)]
    ones = jnp.ones((count, size), BF16)
    sums = []
    for h, cut in enumerate(cuts):
        rows = jnp.concatenate([x[h * length : (h + 1) * length] for x in apart], axis=0)
        extended = jnp.concatenate([values[:, cut], ones], axis=1)
        sums.append(jnp.dot(rows, extended, preferred_element_type=F32))
    rows = []
    for both in sums:
        both = both.astype(BF16).astype(F32)
        total = both[:length]
        for b in range(1, slots):
            total = total + both[b * length : (b + 1) * length]
        rows.append(total[:, :size] / total[:, size:])
    rows = jnp.concatenate(rows, axis=1)
    pieces = [rows[b * tokens : (b + 1) * tokens] for b in range(slots)]
    for b in range(slots):
        outs[b][:length] = swapped(pieces, b).astype(BF16)
        outs[b][length:] = jnp.concatenate([fresh_keys[own[b]], fresh_values[own[b]]], axis=0).astype(BF16)


def partial_kernel(weight_ref, *refs, numbers, rows, before):
    columns = weight_ref.shape[1]
    mine = lax.axis_index("seq")
    total = refs[len(numbers)][...] if before else None
    for ref, b in zip(refs[: len(numbers)], numbers, strict=True):
        start = pl.multiple_of((mine ^ b) * columns, columns)
        term = jnp.dot(ref[:rows], weight_ref[pl.ds(start, columns), :], preferred_element_type=F32)
        total = term if total is None else total + term
    refs[-1][...] = total


def output_kernel(gate_ref, held_ref, weight_ref, total_ref, attention_ref, *outs, number, tokens, turns):
    columns = weight_ref.shape[1]
    start = pl.multiple_of((lax.axis_index("seq") ^ number) * columns, columns)
    rows = total_ref.shape[0]
    total = total_ref[...] + jnp.dot(
        attention_ref[:rows], weight_ref[pl.ds(start, columns), :], preferred_element_type=F32
    )
    block = held_ref[...].astype(F32) + gate_ref[...] * total.astype(BF16).astype(F32)
    pieces = [block[b * tokens : (b + 1) * tokens] for b in range(len(outs))]
    even = lax.rem(lax.axis_index("section"), 2) == 0
    for out, (b, c) in zip(outs, turns, strict=True):
        out[...] = jnp.where(even, pieces[b], pieces[c]).astype(BF16)


def place_kernel(*refs, slots, turns):
    out_ref, refs = refs[slots], refs[:slots][::-1]
    columns = refs[0].shape[1]
    mine, sections = lax.axis_index("seq"), lax.axis_size("section")
    even = lax.rem(lax.axis_index("section") + (sections - 1), sections) % 2 == 0
    for ref, (b, c) in zip(refs, turns, strict=True):
        start = pl.multiple_of((mine ^ jnp.where(even, b, c)) * columns, columns)
        out_ref[0, :, pl.ds(start, columns)] = ref[...]


def place_kv_kernel(*refs, slots, tokens):
    out_ref, refs = refs[slots], refs[:slots][::-1]
    columns = refs[0].shape[1]
    mine = lax.axis_index("seq")
    for b in range(slots):
        start = pl.multiple_of((mine ^ b) * columns, columns)
        piece = refs[b][slots * tokens :].astype(F32)
        both = jnp.stack([piece[:tokens], piece[tokens:]], axis=1)
        out_ref[0, :, :, pl.ds(start, columns)] = both.astype(BF16)


def call(kernel, flops, out_shape, operands, scratch=(), **sizes):
    return pl.pallas_call(
        functools.partial(kernel, **sizes),
        out_shape=out_shape,
        in_specs=[VMEM] * len(operands),
        out_specs=jax.tree.map(lambda _: VMEM, out_shape),
        scratch_shapes=scratch,
        compiler_params=pltpu.CompilerParams(vmem_limit_bytes=16 * 2**20),
        cost_estimate=pl.CostEstimate(flops=int(flops), transcendentals=0, bytes_accessed=2**20),
    )(*operands)


def apart(slots):
    return APART if slots > 2 else ()


def body_by_heads(hidden, kv_cache, w_qkv, w_out, norm_gain, modulation, patch_order, timestep):
    slots, sections = lax.axis_size("seq"), lax.axis_size("section")
    tokens, width = hidden.shape[1:]
    patches = kv_cache.shape[1]
    columns, size = w_qkv.shape[3], norm_gain.shape[2]
    heads, stale, rows = columns // size, (patches - 1) * tokens, slots * tokens
    split = apart(slots)
    turns = TURNS if slots == 4 else [(b, b) for b in range(slots)]

    def array(*shape, dtype=BF16):
        return jax.ShapeDtypeStruct(shape, dtype)

    def moved(array, number):
        return lax.ppermute(array, "seq", [(j, j ^ number) for j in range(slots)])

    def onward(array, turn):
        pairs = [
            (j * sections + s, (j ^ turn[s % 2]) * sections + (s + 1) % sections)
            for j in range(slots)
            for s in range(sections)
        ]
        return lax.ppermute(array, ("seq", "section"), pairs)

    def exchanged(arrays):
        return [arrays[0]] + [moved(arrays[b], b) for b in range(1, slots)]

    own = hidden[0]
    alone = {b: moved(own, b) for b in split}
    ahead = call(ahead_kernel, 5e9, array(8, 128, dtype=F32), [])
    packed = {}
    far = tuple(b for b in range(1, slots) if b not in split)
    for numbers in (far, (0, *split)):
        outs = call(
            pack_kernel,
            5e9,
            [array(2 * stale + (rows if b in far else 0), columns) for b in numbers],
            [patch_order[None], ahead, own, kv_cache],
            numbers=numbers,
            slots=slots,
            patches=patches,
            columns=columns,
            split=split,
        )
        packed |= dict(zip(numbers, outs, strict=True))
    packed = [packed[b] for b in range(slots)]
    old = exchanged(packed)
    inputs = [own] + [alone[b] if b in split else old[b] for b in range(1, slots)]
    weights = jnp.transpose(w_qkv[0], (1, 0, 2))
    queries, keys, normed, held, gate = call(
        project_kernel,
        2e9,
        [
            array(rows, columns),
            array(rows, columns),
            array(rows, width),
            array(rows, columns),
            array(1, columns, dtype=F32),
        ],
        [timestep[None], jnp.transpose(modulation[0], (1, 0, 2)), norm_gain[0], weights, *inputs[::-1]],
        scratch=[pltpu.VMEM((rows, width), F32)],
        slots=slots,
        tokens=tokens,
        heads=heads,
        size=size,
        stale=stale,
    )
    ordered = call(
        attend_kernel,
        2e9,
        [array(rows + 2 * tokens, columns)] * slots,
        [queries, keys, normed, weights, *old[::-1]],
        slots=slots,
        tokens=tokens,
        stale=stale,
        heads=heads,
        size=size,
    )
    attention = exchanged(ordered)
    out_weights = w_out[0]
    groups = [(0, 2), (3,)]
    total = []
    for numbers in groups:
        operands = [out_weights] + [attention[b] for b in numbers] + total
        total = [
            call(
                partial_kernel,
                1e9,
                array(rows, columns, dtype=F32),
                operands,
                numbers=numbers,
                rows=rows,
                before=bool(total),
            )
        ]
    pieces = call(
        output_kernel,
        2e9,
        [array(tokens, columns)] * slots,
        [gate, held, out_weights, *total, attention[1]],
        number=1,
        tokens=tokens,
        turns=turns,
    )
    arrived = [onward(piece, turn) for piece, turn in zip(pieces, turns, strict=True)]
    fresh_kv = call(place_kv_kernel, 1e9, array(1, tokens, 2, width), attention[::-1], slots=slots, tokens=tokens)
    next_hidden = call(place_kernel, 1e9, array(1, tokens, width), arrived[::-1], slots=slots, turns=turns)
    return (next_hidden, fresh_kv)


def body_by_tokens(hidden, kv_cache, w_qkv, w_out, norm_gain, modulation, patch_order, timestep):
    section_index = lax.axis_index("section")
    patch_index = lax.dynamic_index_in_dim(patch_order, section_index, 0, keepdims=False)
    step_index = lax.dynamic_index_in_dim(timestep, section_index, 0, keepdims=False)
    modulate = lax.dynamic_index_in_dim(modulation[0], step_index, 0, keepdims=False)
    model_width = hidden.shape[2]
    head_size = norm_gain.shape[2]
    head_count = model_width // head_size
    col_width = w_qkv.shape[3]
    rows_in = hidden[0].astype(jnp.float32)
    own_count = rows_in.shape[0]
    normed = (layer_norm(rows_in) * (1.0 + modulate[1]) + modulate[0]).astype(jnp.bfloat16)
    w_local = w_qkv[0].reshape(model_width, 3 * col_width)
    projected = jnp.dot(
        lax.all_gather(normed, "seq", axis=0, tiled=True),
        w_local,
        preferred_element_type=jnp.float32,
    ).astype(jnp.bfloat16)
    patch_len = projected.shape[0]
    projected = projected.reshape(patch_len, 3, col_width)
    query_cols = lax.all_gather(projected[:, 0], "seq", axis=1, tiled=True)
    kv_rows = lax.all_to_all(projected[:, 1:], "seq", split_axis=0, concat_axis=2, tiled=True)
    queries = head_norm(
        query_cols.astype(jnp.float32).reshape(patch_len, head_count, head_size), norm_gain[0, 0]
    ).astype(jnp.bfloat16)
    key_rows = head_norm(
        kv_rows[:, 0].astype(jnp.float32).reshape(own_count, head_count, head_size), norm_gain[0, 1]
    ).astype(jnp.bfloat16)
    fresh = jnp.stack([key_rows.reshape(own_count, model_width), kv_rows[:, 1]], axis=1)
    zero = jnp.zeros((), jnp.int32)
    local_kv = lax.dynamic_update_slice(kv_cache[0], fresh[None], (patch_index, zero, zero, zero))
    patch_count = local_kv.shape[0]
    local_keys = local_kv[:, :, 0].reshape(patch_count * own_count, head_count, head_size)
    local_values = local_kv[:, :, 1].reshape(patch_count * own_count, head_count, head_size)
    scores = jnp.einsum(
        "thd,shd->hts", queries, local_keys, preferred_element_type=jnp.float32
    ) / math.sqrt(head_size)
    row_top = lax.pmax(jnp.max(scores, axis=-1), "seq")
    weights = jnp.exp(scores - row_top[:, :, None]).astype(jnp.bfloat16)
    denominator = jnp.sum(weights, axis=-1, dtype=jnp.float32).T
    numerator = jnp.einsum(
        "hts,shd->thd", weights, local_values, preferred_element_type=jnp.float32
    ).reshape(patch_len, model_width)
    totals, counts = (
        lax.psum(numerator.astype(jnp.bfloat16), "seq").astype(jnp.float32),
        lax.psum(denominator.astype(jnp.bfloat16), "seq").astype(jnp.float32),
    )
    attention = (totals.reshape(patch_len, head_count, head_size) / counts[:, :, None]).astype(
        jnp.bfloat16
    )
    attention = attention.reshape(patch_len, model_width)
    out_cols = jnp.dot(attention, w_out[0], preferred_element_type=jnp.float32).astype(jnp.bfloat16)
    out_rows = lax.all_to_all(out_cols, "seq", split_axis=0, concat_axis=1, tiled=True)
    block = (rows_in + modulate[2] * out_rows.astype(jnp.float32)).astype(jnp.bfloat16)
    arrived = passed_along(block, "section", 1)
    return (arrived[None], fresh[None])


def body(hidden, kv_cache, w_qkv, w_out, norm_gain, modulation, patch_order, timestep):
    count = lax.axis_size("seq")
    whole_heads = w_qkv.shape[3] % norm_gain.shape[2] == 0
    chosen = body_by_heads if whole_heads and count & (count - 1) == 0 else body_by_tokens
    return chosen(hidden, kv_cache, w_qkv, w_out, norm_gain, modulation, patch_order, timestep)


def solution(mesh):
    return jax.shard_map(
        body,
        mesh=mesh,
        in_specs=(
            P("section", ("groups", "seq"), None),
            P("section", None, ("groups", "seq"), None, None),
            P("section", None, None, "seq"),
            P("section", None, "seq"),
            P("section", None, None),
            P("section", None, None, None),
            P("groups"),
            P("groups"),
        ),
        out_specs=(
            P("section", ("groups", "seq"), None),
            P("section", ("groups", "seq"), None, None),
        ),
        check_vma=False,
    )
```

```python
import functools
import math

import jax
import jax.numpy as jnp
from jax import lax
from jax.experimental import pallas as pl
from jax.experimental.pallas import tpu as pltpu
from jax.sharding import PartitionSpec as P


APART = (1, 2)
TURNS = (
    ((3, 2, 1, 0), (1, 2, 0, 3)),
    ((0, 1, 2, 3), (2, 3, 1, 0)),
    ((1, 3, 0, 2), (3, 0, 2, 1)),
    ((2, 0, 3, 1), (0, 1, 3, 2)),
)

F32 = jnp.float32
BF16 = jnp.bfloat16
VMEM = pl.BlockSpec(memory_space=pltpu.VMEM)


def passed_along(array, axis, by):
    count = lax.axis_size(axis)
    return lax.ppermute(array, axis, [(i, (i + by) % count) for i in range(count)])


def layer_norm(values_in):
    center = values_in - jnp.mean(values_in, axis=-1, keepdims=True)
    spread = jnp.mean(center * center, axis=-1, keepdims=True)
    return center * lax.rsqrt(spread + 1e-06)


def head_norm(values_in, gain):
    square = jnp.mean(values_in * values_in, axis=-1, keepdims=True)
    return values_in * lax.rsqrt(square + 1e-06) * gain


def swapped(slots, number):
    return jnp.concatenate([slots[b ^ number] for b in range(len(slots))], axis=0)


def ahead_kernel(out_ref):
    out_ref[...] = jnp.zeros_like(out_ref)


def entry(ref):
    lane = lax.broadcasted_iota(jnp.int32, ref.shape, 1)
    mine = lane == lax.axis_index("section")
    return jnp.sum(jnp.where(mine, ref[...], 0).astype(F32), axis=1, keepdims=True)


def pack_kernel(order_ref, _, hidden_ref, cache_ref, *outs, numbers, slots, patches, columns, split):
    mine = lax.axis_index("seq")
    patch = entry(order_ref)
    for out, b in zip(outs, numbers, strict=True):
        start = pl.multiple_of((mine ^ b) * columns, columns)
        both = [cache_ref[0, p, :, :, pl.ds(start, columns)].astype(F32) for p in range(patches)]
        both = [x[:, part] for part in range(2) for x in both]
        stale = []
        for part in range(2):
            for i in range(part * patches, (part + 1) * patches - 1):
                stale.append(jnp.where(patch > i - part * patches, both[i], both[i + 1]))
        stale = jnp.concatenate(stale, axis=0).astype(BF16)
        out[: stale.shape[0]] = stale
        if b and b not in split:
            hidden = hidden_ref[...].astype(F32)
            hidden = [hidden[:, c * columns : (c + 1) * columns] for c in range(slots)]
            out[stale.shape[0] :] = jnp.concatenate(hidden, axis=0).astype(BF16)


def project_kernel(step_ref, mod_ref, gain_ref, weight_ref, *refs, slots, tokens, heads, size, stale):
    hidden_refs = refs[:slots][::-1]
    q_ref, k_ref, normed_ref, held_ref, gate_ref, scratch = refs[slots:]
    mine = lax.axis_index("seq")
    columns, length = heads * size, slots * tokens
    step = lax.broadcasted_iota(jnp.int32, (mod_ref.shape[1], 1), 0).astype(F32) == entry(step_ref)
    modulate = [jnp.sum(jnp.where(step, mod_ref[i], 0.0), axis=0, keepdims=True) for i in range(2)]
    start = pl.multiple_of(mine * columns, columns)
    rows = []
    for ref in hidden_refs:
        if ref.shape[0] == tokens:
            rows.append(ref[...].astype(F32))
        else:
            cut = ref[2 * stale :].astype(F32)
            rows.append(jnp.concatenate([cut[c * tokens : (c + 1) * tokens] for c in range(slots)], axis=1))
    rows = jnp.concatenate(rows, axis=0)
    normed = (layer_norm(rows) * (1.0 + modulate[1]) + modulate[0]).astype(BF16)
    normed_ref[...] = normed
    for part, out in enumerate((q_ref, k_ref)):
        dotted = jnp.dot(normed, weight_ref[part], preferred_element_type=F32).astype(BF16).astype(F32)
        stacked = jnp.concatenate([dotted[:, h * size : (h + 1) * size] for h in range(heads)], axis=0)
        stacked = head_norm(stacked, gain_ref[pl.ds(part, 1), :]).astype(BF16)
        for h in range(heads):
            out[:, h * size : (h + 1) * size] = stacked[h * length : (h + 1) * length]
    scratch[...] = rows
    held_ref[...] = scratch[:, pl.ds(start, columns)].astype(BF16)
    gates = jnp.where(step, mod_ref[2, :, pl.ds(start, columns)], 0.0)
    gate_ref[...] = jnp.sum(gates, axis=0, keepdims=True)


def attend_kernel(q_ref, k_ref, normed_ref, weight_ref, *refs, slots, tokens, stale, heads, size):
    old, outs = refs[:slots][::-1], refs[slots:]
    old = [r[: 2 * stale].astype(F32) for r in old]
    fresh_keys = k_ref[...].astype(F32)
    own = [slice(b * tokens, (b + 1) * tokens) for b in range(slots)]
    per = stale + tokens
    count = slots * per
    keys = jnp.concatenate([x for b in range(slots) for x in (old[b][:stale], fresh_keys[own[b]])], axis=0).astype(BF16)
    queries = q_ref[...]
    length = queries.shape[0]
    cuts = [slice(h * size, (h + 1) * size) for h in range(heads)]
    dims = (((1,), (1,)), ((), ()))
    scores = [lax.dot_general(queries[:, cut], keys[:, cut], dims, preferred_element_type=F32) for cut in cuts]
    fresh_values = jnp.dot(normed_ref[...], weight_ref[2], preferred_element_type=F32).astype(BF16).astype(F32)
    scores = jnp.concatenate(scores, axis=0) / math.sqrt(size)
    top = jnp.max(scores, axis=-1, keepdims=True)
    weights = jnp.exp(scores - top).astype(BF16).astype(F32)
    values = [x for b in range(slots) for x in (old[b][stale:], fresh_values[own[b]])]
    values = jnp.concatenate(values, axis=0).astype(BF16)
    lane = lax.broadcasted_iota(jnp.int32, weights.shape, 1)
    apart = [jnp.where((lane >= b * per) & (lane < (b + 1) * per), weights, 0.0).astype(BF16) for b in range(slots)]
    ones = jnp.ones((count, size), BF16)
    sums = []
    for h, cut in enumerate(cuts):
        rows = jnp.concatenate([x[h * length : (h + 1) * length] for x in apart], axis=0)
        extended = jnp.concatenate([values[:, cut], ones], axis=1)
        sums.append(jnp.dot(rows, extended, preferred_element_type=F32))
    rows = []
    for both in sums:
        both = both.astype(BF16).astype(F32)
        total = both[:length]
        for b in range(1, slots):
            total = total + both[b * length : (b + 1) * length]
        rows.append(total[:, :size] / total[:, size:])
    rows = jnp.concatenate(rows, axis=1)
    pieces = [rows[b * tokens : (b + 1) * tokens] for b in range(slots)]
    for b in range(slots):
        outs[b][:length] = swapped(pieces, b).astype(BF16)
        outs[b][length:] = jnp.concatenate([fresh_keys[own[b]], fresh_values[own[b]]], axis=0).astype(BF16)


def partial_kernel(weight_ref, *refs, numbers, rows, before):
    columns = weight_ref.shape[1]
    mine = lax.axis_index("seq")
    total = refs[len(numbers)][...] if before else None
    for ref, b in zip(refs[: len(numbers)], numbers, strict=True):
        start = pl.multiple_of((mine ^ b) * columns, columns)
        term = jnp.dot(ref[:rows], weight_ref[pl.ds(start, columns), :], preferred_element_type=F32)
        total = term if total is None else total + term
    refs[-1][...] = total


def peer(turn, section):
    mine = lax.axis_index("seq")
    entries = []
    for targets in turn:
        found = targets[0]
        for j in range(1, len(targets)):
            found = jnp.where(mine == j, targets[j], found)
        entries.append(found)
    return jnp.where(lax.rem(section, 2) == 0, entries[0], entries[1])


def output_kernel(gate_ref, held_ref, weight_ref, total_ref, attention_ref, *outs, number, tokens, turns):
    columns = weight_ref.shape[1]
    start = pl.multiple_of((lax.axis_index("seq") ^ number) * columns, columns)
    rows = total_ref.shape[0]
    total = total_ref[...] + jnp.dot(
        attention_ref[:rows], weight_ref[pl.ds(start, columns), :], preferred_element_type=F32
    )
    block = held_ref[...].astype(F32) + gate_ref[...] * total.astype(BF16).astype(F32)
    pieces = [block[b * tokens : (b + 1) * tokens] for b in range(len(outs))]
    mine = lax.axis_index("seq")
    for out, turn in zip(outs, turns, strict=True):
        slot = mine ^ peer(turn, lax.axis_index("section"))
        piece = pieces[0]
        for b in range(1, len(pieces)):
            piece = jnp.where(slot == b, pieces[b], piece)
        out[...] = piece.astype(BF16)


def place_kernel(*refs, slots, turns):
    out_ref, refs = refs[slots], refs[:slots][::-1]
    columns = refs[0].shape[1]
    sections = lax.axis_size("section")
    before = lax.rem(lax.axis_index("section") + (sections - 1), sections)
    for ref, turn in zip(refs, turns, strict=True):
        back = [[targets.index(j) for j in range(slots)] for targets in turn]
        start = pl.multiple_of(peer(back, before) * columns, columns)
        out_ref[0, :, pl.ds(start, columns)] = ref[...]


def place_kv_kernel(*refs, slots, tokens):
    out_ref, refs = refs[slots], refs[:slots][::-1]
    columns = refs[0].shape[1]
    mine = lax.axis_index("seq")
    for b in range(slots):
        start = pl.multiple_of((mine ^ b) * columns, columns)
        piece = refs[b][slots * tokens :].astype(F32)
        both = jnp.stack([piece[:tokens], piece[tokens:]], axis=1)
        out_ref[0, :, :, pl.ds(start, columns)] = both.astype(BF16)


def call(kernel, flops, out_shape, operands, scratch=(), **sizes):
    return pl.pallas_call(
        functools.partial(kernel, **sizes),
        out_shape=out_shape,
        in_specs=[VMEM] * len(operands),
        out_specs=jax.tree.map(lambda _: VMEM, out_shape),
        scratch_shapes=scratch,
        compiler_params=pltpu.CompilerParams(vmem_limit_bytes=16 * 2**20),
        cost_estimate=pl.CostEstimate(flops=int(flops), transcendentals=0, bytes_accessed=2**20),
    )(*operands)


def apart(slots):
    return APART if slots > 2 else ()


def body_by_heads(hidden, kv_cache, w_qkv, w_out, norm_gain, modulation, patch_order, timestep):
    slots, sections = lax.axis_size("seq"), lax.axis_size("section")
    tokens, width = hidden.shape[1:]
    patches = kv_cache.shape[1]
    columns, size = w_qkv.shape[3], norm_gain.shape[2]
    heads, stale, rows = columns // size, (patches - 1) * tokens, slots * tokens
    split = apart(slots)
    turns = TURNS if slots == 4 else [([j ^ b for j in range(slots)],) * 2 for b in range(slots)]

    def array(*shape, dtype=BF16):
        return jax.ShapeDtypeStruct(shape, dtype)

    def moved(array, number):
        return lax.ppermute(array, "seq", [(j, j ^ number) for j in range(slots)])

    def onward(array, number):
        turn = turns[number]
        pairs = [
            (j * sections + s, turn[s % 2][j] * sections + (s + 1) % sections)
            for j in range(slots)
            for s in range(sections)
        ]
        return lax.ppermute(array, ("seq", "section"), pairs)

    def exchanged(arrays):
        return [arrays[0]] + [moved(arrays[b], b) for b in range(1, slots)]

    own = hidden[0]
    alone = {b: moved(own, b) for b in split}
    ahead = call(ahead_kernel, 5e9, array(8, 128, dtype=F32), [])
    packed = {}
    far = tuple(b for b in range(1, slots) if b not in split)
    for numbers in (far, (0, *split)):
        outs = call(
            pack_kernel,
            5e9,
            [array(2 * stale + (rows if b in far else 0), columns) for b in numbers],
            [patch_order[None], ahead, own, kv_cache],
            numbers=numbers,
            slots=slots,
            patches=patches,
            columns=columns,
            split=split,
        )
        packed |= dict(zip(numbers, outs, strict=True))
    packed = [packed[b] for b in range(slots)]
    old = exchanged(packed)
    inputs = [own] + [alone[b] if b in split else old[b] for b in range(1, slots)]
    weights = jnp.transpose(w_qkv[0], (1, 0, 2))
    queries, keys, normed, held, gate = call(
        project_kernel,
        2e9,
        [
            array(rows, columns),
            array(rows, columns),
            array(rows, width),
            array(rows, columns),
            array(1, columns, dtype=F32),
        ],
        [timestep[None], jnp.transpose(modulation[0], (1, 0, 2)), norm_gain[0], weights, *inputs[::-1]],
        scratch=[pltpu.VMEM((rows, width), F32)],
        slots=slots,
        tokens=tokens,
        heads=heads,
        size=size,
        stale=stale,
    )
    ordered = call(
        attend_kernel,
        2e9,
        [array(rows + 2 * tokens, columns)] * slots,
        [queries, keys, normed, weights, *old[::-1]],
        slots=slots,
        tokens=tokens,
        stale=stale,
        heads=heads,
        size=size,
    )
    attention = exchanged(ordered)
    out_weights = w_out[0]
    groups = [(0, 2), (3,)]
    total = []
    for numbers in groups:
        operands = [out_weights] + [attention[b] for b in numbers] + total
        total = [
            call(
                partial_kernel,
                1e9,
                array(rows, columns, dtype=F32),
                operands,
                numbers=numbers,
                rows=rows,
                before=bool(total),
            )
        ]
    pieces = call(
        output_kernel,
        2e9,
        [array(tokens, columns)] * slots,
        [gate, held, out_weights, *total, attention[1]],
        number=1,
        tokens=tokens,
        turns=turns,
    )
    arrived = [onward(piece, number) for number, piece in enumerate(pieces)]
    fresh_kv = call(place_kv_kernel, 1e9, array(1, tokens, 2, width), attention[::-1], slots=slots, tokens=tokens)
    next_hidden = call(place_kernel, 1e9, array(1, tokens, width), arrived[::-1], slots=slots, turns=turns)
    return (next_hidden, fresh_kv)


def body_by_tokens(hidden, kv_cache, w_qkv, w_out, norm_gain, modulation, patch_order, timestep):
    section_index = lax.axis_index("section")
    patch_index = lax.dynamic_index_in_dim(patch_order, section_index, 0, keepdims=False)
    step_index = lax.dynamic_index_in_dim(timestep, section_index, 0, keepdims=False)
    modulate = lax.dynamic_index_in_dim(modulation[0], step_index, 0, keepdims=False)
    model_width = hidden.shape[2]
    head_size = norm_gain.shape[2]
    head_count = model_width // head_size
    col_width = w_qkv.shape[3]
    rows_in = hidden[0].astype(jnp.float32)
    own_count = rows_in.shape[0]
    normed = (layer_norm(rows_in) * (1.0 + modulate[1]) + modulate[0]).astype(jnp.bfloat16)
    w_local = w_qkv[0].reshape(model_width, 3 * col_width)
    projected = jnp.dot(
        lax.all_gather(normed, "seq", axis=0, tiled=True),
        w_local,
        preferred_element_type=jnp.float32,
    ).astype(jnp.bfloat16)
    patch_len = projected.shape[0]
    projected = projected.reshape(patch_len, 3, col_width)
    query_cols = lax.all_gather(projected[:, 0], "seq", axis=1, tiled=True)
    kv_rows = lax.all_to_all(projected[:, 1:], "seq", split_axis=0, concat_axis=2, tiled=True)
    queries = head_norm(
        query_cols.astype(jnp.float32).reshape(patch_len, head_count, head_size), norm_gain[0, 0]
    ).astype(jnp.bfloat16)
    key_rows = head_norm(
        kv_rows[:, 0].astype(jnp.float32).reshape(own_count, head_count, head_size), norm_gain[0, 1]
    ).astype(jnp.bfloat16)
    fresh = jnp.stack([key_rows.reshape(own_count, model_width), kv_rows[:, 1]], axis=1)
    zero = jnp.zeros((), jnp.int32)
    local_kv = lax.dynamic_update_slice(kv_cache[0], fresh[None], (patch_index, zero, zero, zero))
    patch_count = local_kv.shape[0]
    local_keys = local_kv[:, :, 0].reshape(patch_count * own_count, head_count, head_size)
    local_values = local_kv[:, :, 1].reshape(patch_count * own_count, head_count, head_size)
    scores = jnp.einsum(
        "thd,shd->hts", queries, local_keys, preferred_element_type=jnp.float32
    ) / math.sqrt(head_size)
    row_top = lax.pmax(jnp.max(scores, axis=-1), "seq")
    weights = jnp.exp(scores - row_top[:, :, None]).astype(jnp.bfloat16)
    denominator = jnp.sum(weights, axis=-1, dtype=jnp.float32).T
    numerator = jnp.einsum(
        "hts,shd->thd", weights, local_values, preferred_element_type=jnp.float32
    ).reshape(patch_len, model_width)
    totals, counts = (
        lax.psum(numerator.astype(jnp.bfloat16), "seq").astype(jnp.float32),
        lax.psum(denominator.astype(jnp.bfloat16), "seq").astype(jnp.float32),
    )
    attention = (totals.reshape(patch_len, head_count, head_size) / counts[:, :, None]).astype(
        jnp.bfloat16
    )
    attention = attention.reshape(patch_len, model_width)
    out_cols = jnp.dot(attention, w_out[0], preferred_element_type=jnp.float32).astype(jnp.bfloat16)
    out_rows = lax.all_to_all(out_cols, "seq", split_axis=0, concat_axis=1, tiled=True)
    block = (rows_in + modulate[2] * out_rows.astype(jnp.float32)).astype(jnp.bfloat16)
    arrived = passed_along(block, "section", 1)
    return (arrived[None], fresh[None])


def body(hidden, kv_cache, w_qkv, w_out, norm_gain, modulation, patch_order, timestep):
    count = lax.axis_size("seq")
    whole_heads = w_qkv.shape[3] % norm_gain.shape[2] == 0
    chosen = body_by_heads if whole_heads and count & (count - 1) == 0 else body_by_tokens
    return chosen(hidden, kv_cache, w_qkv, w_out, norm_gain, modulation, patch_order, timestep)


def solution(mesh):
    return jax.shard_map(
        body,
        mesh=mesh,
        in_specs=(
            P("section", ("groups", "seq"), None),
            P("section", None, ("groups", "seq"), None, None),
            P("section", None, None, "seq"),
            P("section", None, "seq"),
            P("section", None, None),
            P("section", None, None, None),
            P("groups"),
            P("groups"),
        ),
        out_specs=(
            P("section", ("groups", "seq"), None),
            P("section", ("groups", "seq"), None, None),
        ),
        check_vma=False,
    )
```

```python
import functools
import math

import jax
import jax.numpy as jnp
from jax import lax
from jax.experimental import pallas as pl
from jax.experimental.pallas import tpu as pltpu
from jax.sharding import PartitionSpec as P


APART = (1, 2)
TURNS = (
    ((3, 2, 1, 0), (1, 2, 0, 3)),
    ((0, 1, 2, 3), (2, 3, 1, 0)),
    ((1, 3, 0, 2), (3, 0, 2, 1)),
    ((2, 0, 3, 1), (0, 1, 3, 2)),
)

F32 = jnp.float32
BF16 = jnp.bfloat16
VMEM = pl.BlockSpec(memory_space=pltpu.VMEM)


def passed_along(array, axis, by):
    count = lax.axis_size(axis)
    return lax.ppermute(array, axis, [(i, (i + by) % count) for i in range(count)])


def layer_norm(values_in):
    center = values_in - jnp.mean(values_in, axis=-1, keepdims=True)
    spread = jnp.mean(center * center, axis=-1, keepdims=True)
    return center * lax.rsqrt(spread + 1e-06)


def head_norm(values_in, gain):
    square = jnp.mean(values_in * values_in, axis=-1, keepdims=True)
    return values_in * lax.rsqrt(square + 1e-06) * gain


def swapped(slots, number):
    return jnp.concatenate([slots[b ^ number] for b in range(len(slots))], axis=0)


def ahead_kernel(out_ref):
    out_ref[...] = jnp.zeros_like(out_ref)


def entry(ref):
    lane = lax.broadcasted_iota(jnp.int32, ref.shape, 1)
    mine = lane == lax.axis_index("section")
    return jnp.sum(jnp.where(mine, ref[...], 0).astype(F32), axis=1, keepdims=True)


def pack_kernel(order_ref, _, hidden_ref, cache_ref, *outs, numbers, slots, patches, columns, split):
    mine = lax.axis_index("seq")
    patch = entry(order_ref)
    for out, b in zip(outs, numbers, strict=True):
        start = pl.multiple_of((mine ^ b) * columns, columns)
        both = [cache_ref[0, p, :, :, pl.ds(start, columns)].astype(F32) for p in range(patches)]
        both = [x[:, part] for part in range(2) for x in both]
        stale = []
        for part in range(2):
            for i in range(part * patches, (part + 1) * patches - 1):
                stale.append(jnp.where(patch > i - part * patches, both[i], both[i + 1]))
        stale = jnp.concatenate(stale, axis=0).astype(BF16)
        out[: stale.shape[0]] = stale
        if b and b not in split:
            hidden = hidden_ref[...].astype(F32)
            hidden = [hidden[:, c * columns : (c + 1) * columns] for c in range(slots)]
            out[stale.shape[0] :] = jnp.concatenate(hidden, axis=0).astype(BF16)


def project_kernel(step_ref, mod_ref, gain_ref, weight_ref, *refs, slots, tokens, heads, size, stale):
    hidden_refs = refs[:slots][::-1]
    q_ref, k_ref, v_ref, held_ref, gate_ref, scratch = refs[slots:]
    mine = lax.axis_index("seq")
    columns, length = heads * size, slots * tokens
    step = lax.broadcasted_iota(jnp.int32, (mod_ref.shape[1], 1), 0).astype(F32) == entry(step_ref)
    modulate = [jnp.sum(jnp.where(step, mod_ref[i], 0.0), axis=0, keepdims=True) for i in range(2)]
    start = pl.multiple_of(mine * columns, columns)
    rows = []
    for ref in hidden_refs:
        if ref.shape[0] == tokens:
            rows.append(ref[...].astype(F32))
        else:
            cut = ref[2 * stale :].astype(F32)
            rows.append(jnp.concatenate([cut[c * tokens : (c + 1) * tokens] for c in range(slots)], axis=1))
    rows = jnp.concatenate(rows, axis=0)
    normed = (layer_norm(rows) * (1.0 + modulate[1]) + modulate[0]).astype(BF16)
    for part, out in enumerate((q_ref, k_ref)):
        dotted = jnp.dot(normed, weight_ref[part], preferred_element_type=F32).astype(BF16).astype(F32)
        stacked = jnp.concatenate([dotted[:, h * size : (h + 1) * size] for h in range(heads)], axis=0)
        stacked = head_norm(stacked, gain_ref[pl.ds(part, 1), :]).astype(BF16)
        for h in range(heads):
            out[:, h * size : (h + 1) * size] = stacked[h * length : (h + 1) * length]
    v_ref[...] = jnp.dot(normed, weight_ref[2], preferred_element_type=F32).astype(BF16)
    scratch[...] = rows
    held_ref[...] = scratch[:, pl.ds(start, columns)].astype(BF16)
    gates = jnp.where(step, mod_ref[2, :, pl.ds(start, columns)], 0.0)
    gate_ref[...] = jnp.sum(gates, axis=0, keepdims=True)


def attend_kernel(q_ref, k_ref, v_ref, *refs, slots, tokens, stale, heads, size):
    old, outs = refs[:slots][::-1], refs[slots:]
    old = [r[: 2 * stale].astype(F32) for r in old]
    fresh_keys = k_ref[...].astype(F32)
    own = [slice(b * tokens, (b + 1) * tokens) for b in range(slots)]
    per = stale + tokens
    count = slots * per
    keys = jnp.concatenate([x for b in range(slots) for x in (old[b][:stale], fresh_keys[own[b]])], axis=0).astype(BF16)
    queries = q_ref[...]
    length = queries.shape[0]
    cuts = [slice(h * size, (h + 1) * size) for h in range(heads)]
    dims = (((1,), (1,)), ((), ()))
    scores = [lax.dot_general(queries[:, cut], keys[:, cut], dims, preferred_element_type=F32) for cut in cuts]
    fresh_values = v_ref[...].astype(F32)
    scores = jnp.concatenate(scores, axis=0) / math.sqrt(size)
    top = jnp.max(scores, axis=-1, keepdims=True)
    weights = jnp.exp(scores - top).astype(BF16).astype(F32)
    values = [x for b in range(slots) for x in (old[b][stale:], fresh_values[own[b]])]
    values = jnp.concatenate(values, axis=0).astype(BF16)
    lane = lax.broadcasted_iota(jnp.int32, weights.shape, 1)
    apart = [jnp.where((lane >= b * per) & (lane < (b + 1) * per), weights, 0.0).astype(BF16) for b in range(slots)]
    ones = jnp.ones((count, size), BF16)
    sums = []
    for h, cut in enumerate(cuts):
        rows = jnp.concatenate([x[h * length : (h + 1) * length] for x in apart], axis=0)
        extended = jnp.concatenate([values[:, cut], ones], axis=1)
        sums.append(jnp.dot(rows, extended, preferred_element_type=F32))
    rows = []
    for both in sums:
        both = both.astype(BF16).astype(F32)
        total = both[:length]
        for b in range(1, slots):
            total = total + both[b * length : (b + 1) * length]
        rows.append(total[:, :size] / total[:, size:])
    rows = jnp.concatenate(rows, axis=1)
    pieces = [rows[b * tokens : (b + 1) * tokens] for b in range(slots)]
    for b in range(slots):
        outs[b][:length] = swapped(pieces, b).astype(BF16)
        outs[b][length:] = jnp.concatenate([fresh_keys[own[b]], fresh_values[own[b]]], axis=0).astype(BF16)


def partial_kernel(weight_ref, *refs, numbers, rows, before):
    columns = weight_ref.shape[1]
    mine = lax.axis_index("seq")
    total = refs[len(numbers)][...] if before else None
    for ref, b in zip(refs[: len(numbers)], numbers, strict=True):
        start = pl.multiple_of((mine ^ b) * columns, columns)
        term = jnp.dot(ref[:rows], weight_ref[pl.ds(start, columns), :], preferred_element_type=F32)
        total = term if total is None else total + term
    refs[-1][...] = total


def peer(turn, section):
    mine = lax.axis_index("seq")
    entries = []
    for targets in turn:
        found = targets[0]
        for j in range(1, len(targets)):
            found = jnp.where(mine == j, targets[j], found)
        entries.append(found)
    return jnp.where(lax.rem(section, 2) == 0, entries[0], entries[1])


def output_kernel(gate_ref, held_ref, weight_ref, total_ref, attention_ref, *outs, number, tokens, turns):
    columns = weight_ref.shape[1]
    start = pl.multiple_of((lax.axis_index("seq") ^ number) * columns, columns)
    rows = total_ref.shape[0]
    total = total_ref[...] + jnp.dot(
        attention_ref[:rows], weight_ref[pl.ds(start, columns), :], preferred_element_type=F32
    )
    block = held_ref[...].astype(F32) + gate_ref[...] * total.astype(BF16).astype(F32)
    pieces = [block[b * tokens : (b + 1) * tokens] for b in range(len(outs))]
    mine = lax.axis_index("seq")
    for out, turn in zip(outs, turns, strict=True):
        slot = mine ^ peer(turn, lax.axis_index("section"))
        piece = pieces[0]
        for b in range(1, len(pieces)):
            piece = jnp.where(slot == b, pieces[b], piece)
        out[...] = piece.astype(BF16)


def place_kernel(*refs, slots, turns):
    out_ref, sems, refs = refs[slots], refs[slots + 1], refs[:slots][::-1]
    columns = refs[0].shape[1]
    sections = lax.axis_size("section")
    before = lax.rem(lax.axis_index("section") + (sections - 1), sections)
    copies = []
    for k, (ref, turn) in enumerate(zip(refs, turns, strict=True)):
        back = [[targets.index(j) for j in range(slots)] for targets in turn]
        start = pl.multiple_of(peer(back, before) * columns, columns)
        copies.append(pltpu.make_async_copy(ref, out_ref.at[0, :, pl.ds(start, columns)], sems.at[k]))
    for copy in copies:
        copy.start()
    for copy in copies:
        copy.wait()


def place_kv_kernel(*refs, slots, tokens):
    out_ref, refs = refs[slots], refs[:slots][::-1]
    columns = refs[0].shape[1]
    mine = lax.axis_index("seq")
    for b in range(slots):
        start = pl.multiple_of((mine ^ b) * columns, columns)
        piece = refs[b][slots * tokens :].astype(F32)
        both = jnp.stack([piece[:tokens], piece[tokens:]], axis=1)
        out_ref[0, :, :, pl.ds(start, columns)] = both.astype(BF16)


def call(kernel, flops, out_shape, operands, scratch=(), out_space=pltpu.VMEM, **sizes):
    return pl.pallas_call(
        functools.partial(kernel, **sizes),
        out_shape=out_shape,
        in_specs=[VMEM] * len(operands),
        out_specs=jax.tree.map(lambda _: pl.BlockSpec(memory_space=out_space), out_shape),
        scratch_shapes=scratch,
        compiler_params=pltpu.CompilerParams(vmem_limit_bytes=16 * 2**20),
        cost_estimate=pl.CostEstimate(flops=int(flops), transcendentals=0, bytes_accessed=2**20),
    )(*operands)


def apart(slots):
    return APART if slots > 2 else ()


def body_by_heads(hidden, kv_cache, w_qkv, w_out, norm_gain, modulation, patch_order, timestep):
    slots, sections = lax.axis_size("seq"), lax.axis_size("section")
    tokens, width = hidden.shape[1:]
    patches = kv_cache.shape[1]
    columns, size = w_qkv.shape[3], norm_gain.shape[2]
    heads, stale, rows = columns // size, (patches - 1) * tokens, slots * tokens
    split = apart(slots)
    turns = TURNS if slots == 4 else [([j ^ b for j in range(slots)],) * 2 for b in range(slots)]

    def array(*shape, dtype=BF16):
        return jax.ShapeDtypeStruct(shape, dtype)

    def moved(array, number):
        return lax.ppermute(array, "seq", [(j, j ^ number) for j in range(slots)])

    def onward(array, number):
        turn = turns[number]
        pairs = [
            (j * sections + s, turn[s % 2][j] * sections + (s + 1) % sections)
            for j in range(slots)
            for s in range(sections)
        ]
        return lax.ppermute(array, ("seq", "section"), pairs)

    def exchanged(arrays):
        return [arrays[0]] + [moved(arrays[b], b) for b in range(1, slots)]

    own = hidden[0]
    alone = {b: moved(own, b) for b in split}
    ahead = call(ahead_kernel, 5e9, array(8, 128, dtype=F32), [])
    packed = {}
    far = tuple(b for b in range(1, slots) if b not in split)
    for numbers in (far, (0, *split)):
        outs = call(
            pack_kernel,
            5e9,
            [array(2 * stale + (rows if b in far else 0), columns) for b in numbers],
            [patch_order[None], ahead, own, kv_cache],
            numbers=numbers,
            slots=slots,
            patches=patches,
            columns=columns,
            split=split,
        )
        packed |= dict(zip(numbers, outs, strict=True))
    packed = [packed[b] for b in range(slots)]
    old = exchanged(packed)
    inputs = [own] + [alone[b] if b in split else old[b] for b in range(1, slots)]
    weights = jnp.transpose(w_qkv[0], (1, 0, 2))
    queries, keys, values, held, gate = call(
        project_kernel,
        2e9,
        [
            array(rows, columns),
            array(rows, columns),
            array(rows, columns),
            array(rows, columns),
            array(1, columns, dtype=F32),
        ],
        [timestep[None], jnp.transpose(modulation[0], (1, 0, 2)), norm_gain[0], weights, *inputs[::-1]],
        scratch=[pltpu.VMEM((rows, width), F32)],
        slots=slots,
        tokens=tokens,
        heads=heads,
        size=size,
        stale=stale,
    )
    ordered = call(
        attend_kernel,
        2e9,
        [array(rows + 2 * tokens, columns)] * slots,
        [queries, keys, values, *old[::-1]],
        slots=slots,
        tokens=tokens,
        stale=stale,
        heads=heads,
        size=size,
    )
    attention = exchanged(ordered)
    out_weights = w_out[0]
    groups = [(0, 2), (3,)] if slots == 4 else [(0,)] + [(b,) for b in range(slots - 1, 1, -1)]
    total = []
    for numbers in groups:
        operands = [out_weights] + [attention[b] for b in numbers] + total
        total = [
            call(
                partial_kernel,
                1e9,
                array(rows, columns, dtype=F32),
                operands,
                numbers=numbers,
                rows=rows,
                before=bool(total),
            )
        ]
    pieces = call(
        output_kernel,
        2e9,
        [array(tokens, columns)] * slots,
        [gate, held, out_weights, *total, attention[1]],
        number=1,
        tokens=tokens,
        turns=turns,
    )
    arrived = [onward(piece, number) for number, piece in enumerate(pieces)]
    fresh_kv = call(place_kv_kernel, 1e9, array(1, tokens, 2, width), attention[::-1], slots=slots, tokens=tokens)
    next_hidden = call(
        place_kernel,
        1e9,
        array(1, tokens, width),
        arrived[::-1],
        scratch=[pltpu.SemaphoreType.DMA((slots,))],
        out_space=pl.ANY,
        slots=slots,
        turns=turns,
    )
    return (next_hidden, fresh_kv)


def body_by_tokens(hidden, kv_cache, w_qkv, w_out, norm_gain, modulation, patch_order, timestep):
    section_index = lax.axis_index("section")
    patch_index = lax.dynamic_index_in_dim(patch_order, section_index, 0, keepdims=False)
    step_index = lax.dynamic_index_in_dim(timestep, section_index, 0, keepdims=False)
    modulate = lax.dynamic_index_in_dim(modulation[0], step_index, 0, keepdims=False)
    model_width = hidden.shape[2]
    head_size = norm_gain.shape[2]
    head_count = model_width // head_size
    col_width = w_qkv.shape[3]
    rows_in = hidden[0].astype(jnp.float32)
    own_count = rows_in.shape[0]
    normed = (layer_norm(rows_in) * (1.0 + modulate[1]) + modulate[0]).astype(jnp.bfloat16)
    w_local = w_qkv[0].reshape(model_width, 3 * col_width)
    projected = jnp.dot(
        lax.all_gather(normed, "seq", axis=0, tiled=True),
        w_local,
        preferred_element_type=jnp.float32,
    ).astype(jnp.bfloat16)
    patch_len = projected.shape[0]
    projected = projected.reshape(patch_len, 3, col_width)
    query_cols = lax.all_gather(projected[:, 0], "seq", axis=1, tiled=True)
    kv_rows = lax.all_to_all(projected[:, 1:], "seq", split_axis=0, concat_axis=2, tiled=True)
    queries = head_norm(
        query_cols.astype(jnp.float32).reshape(patch_len, head_count, head_size), norm_gain[0, 0]
    ).astype(jnp.bfloat16)
    key_rows = head_norm(
        kv_rows[:, 0].astype(jnp.float32).reshape(own_count, head_count, head_size), norm_gain[0, 1]
    ).astype(jnp.bfloat16)
    fresh = jnp.stack([key_rows.reshape(own_count, model_width), kv_rows[:, 1]], axis=1)
    zero = jnp.zeros((), jnp.int32)
    local_kv = lax.dynamic_update_slice(kv_cache[0], fresh[None], (patch_index, zero, zero, zero))
    patch_count = local_kv.shape[0]
    local_keys = local_kv[:, :, 0].reshape(patch_count * own_count, head_count, head_size)
    local_values = local_kv[:, :, 1].reshape(patch_count * own_count, head_count, head_size)
    scores = jnp.einsum(
        "thd,shd->hts", queries, local_keys, preferred_element_type=jnp.float32
    ) / math.sqrt(head_size)
    row_top = lax.pmax(jnp.max(scores, axis=-1), "seq")
    weights = jnp.exp(scores - row_top[:, :, None]).astype(jnp.bfloat16)
    denominator = jnp.sum(weights, axis=-1, dtype=jnp.float32).T
    numerator = jnp.einsum(
        "hts,shd->thd", weights, local_values, preferred_element_type=jnp.float32
    ).reshape(patch_len, model_width)
    totals, counts = (
        lax.psum(numerator.astype(jnp.bfloat16), "seq").astype(jnp.float32),
        lax.psum(denominator.astype(jnp.bfloat16), "seq").astype(jnp.float32),
    )
    attention = (totals.reshape(patch_len, head_count, head_size) / counts[:, :, None]).astype(
        jnp.bfloat16
    )
    attention = attention.reshape(patch_len, model_width)
    out_cols = jnp.dot(attention, w_out[0], preferred_element_type=jnp.float32).astype(jnp.bfloat16)
    out_rows = lax.all_to_all(out_cols, "seq", split_axis=0, concat_axis=1, tiled=True)
    block = (rows_in + modulate[2] * out_rows.astype(jnp.float32)).astype(jnp.bfloat16)
    arrived = passed_along(block, "section", 1)
    return (arrived[None], fresh[None])


def body(hidden, kv_cache, w_qkv, w_out, norm_gain, modulation, patch_order, timestep):
    count = lax.axis_size("seq")
    whole_heads = w_qkv.shape[3] % norm_gain.shape[2] == 0
    chosen = body_by_heads if whole_heads and count & (count - 1) == 0 else body_by_tokens
    return chosen(hidden, kv_cache, w_qkv, w_out, norm_gain, modulation, patch_order, timestep)


def solution(mesh):
    return jax.shard_map(
        body,
        mesh=mesh,
        in_specs=(
            P("section", ("groups", "seq"), None),
            P("section", None, ("groups", "seq"), None, None),
            P("section", None, None, "seq"),
            P("section", None, "seq"),
            P("section", None, None),
            P("section", None, None, None),
            P("groups"),
            P("groups"),
        ),
        out_specs=(
            P("section", ("groups", "seq"), None),
            P("section", ("groups", "seq"), None, None),
        ),
        check_vma=False,
    )
```

```python
import functools
import math

import jax
import jax.numpy as jnp
from jax import lax
from jax.experimental import pallas as pl
from jax.experimental.pallas import tpu as pltpu
from jax.sharding import PartitionSpec as P


APART = (1, 2)
TURNS = (
    ((3, 2, 1, 0), (1, 2, 0, 3)),
    ((0, 1, 2, 3), (2, 3, 1, 0)),
    ((1, 3, 0, 2), (3, 0, 2, 1)),
    ((2, 0, 3, 1), (0, 1, 3, 2)),
)

F32 = jnp.float32
BF16 = jnp.bfloat16
VMEM = pl.BlockSpec(memory_space=pltpu.VMEM)


def passed_along(array, axis, by):
    count = lax.axis_size(axis)
    return lax.ppermute(array, axis, [(i, (i + by) % count) for i in range(count)])


def layer_norm(values_in):
    center = values_in - jnp.mean(values_in, axis=-1, keepdims=True)
    spread = jnp.mean(center * center, axis=-1, keepdims=True)
    return center * lax.rsqrt(spread + 1e-06)


def head_norm(values_in, gain):
    square = jnp.mean(values_in * values_in, axis=-1, keepdims=True)
    return values_in * lax.rsqrt(square + 1e-06) * gain


def swapped(slots, number):
    return jnp.concatenate([slots[b ^ number] for b in range(len(slots))], axis=0)


def ahead_kernel(out_ref):
    out_ref[...] = jnp.zeros_like(out_ref)


def entry(ref):
    lane = lax.broadcasted_iota(jnp.int32, ref.shape, 1)
    mine = lane == lax.axis_index("section")
    return jnp.sum(jnp.where(mine, ref[...], 0).astype(F32), axis=1, keepdims=True)


def pack_kernel(order_ref, _, hidden_ref, cache_ref, *outs, numbers, slots, patches, columns, split):
    mine = lax.axis_index("seq")
    patch = entry(order_ref)
    for out, b in zip(outs, numbers, strict=True):
        start = pl.multiple_of((mine ^ b) * columns, columns)
        both = [cache_ref[0, p, :, :, pl.ds(start, columns)].astype(F32) for p in range(patches)]
        both = [x[:, part] for part in range(2) for x in both]
        stale = []
        for part in range(2):
            for i in range(part * patches, (part + 1) * patches - 1):
                stale.append(jnp.where(patch > i - part * patches, both[i], both[i + 1]))
        stale = jnp.concatenate(stale, axis=0).astype(BF16)
        out[: stale.shape[0]] = stale
        if b and b not in split:
            hidden = hidden_ref[...].astype(F32)
            hidden = [hidden[:, c * columns : (c + 1) * columns] for c in range(slots)]
            out[stale.shape[0] :] = jnp.concatenate(hidden, axis=0).astype(BF16)


def project_kernel(step_ref, mod_ref, gain_ref, weight_ref, *refs, slots, tokens, heads, size, stale):
    hidden_refs = refs[:slots][::-1]
    q_ref, k_ref, v_ref, held_ref, gate_ref, scratch = refs[slots:]
    mine = lax.axis_index("seq")
    columns, length = heads * size, slots * tokens
    step = lax.broadcasted_iota(jnp.int32, (mod_ref.shape[1], 1), 0).astype(F32) == entry(step_ref)
    modulate = [jnp.sum(jnp.where(step, mod_ref[i], 0.0), axis=0, keepdims=True) for i in range(2)]
    start = pl.multiple_of(mine * columns, columns)
    rows = []
    for ref in hidden_refs:
        if ref.shape[0] == tokens:
            rows.append(ref[...].astype(F32))
        else:
            cut = ref[2 * stale :].astype(F32)
            rows.append(jnp.concatenate([cut[c * tokens : (c + 1) * tokens] for c in range(slots)], axis=1))
    rows = jnp.concatenate(rows, axis=0)
    normed = (layer_norm(rows) * (1.0 + modulate[1]) + modulate[0]).astype(BF16)
    for part, out in enumerate((q_ref, k_ref)):
        dotted = jnp.dot(normed, weight_ref[part], preferred_element_type=F32).astype(BF16).astype(F32)
        stacked = jnp.concatenate([dotted[:, h * size : (h + 1) * size] for h in range(heads)], axis=0)
        stacked = head_norm(stacked, gain_ref[pl.ds(part, 1), :]).astype(BF16)
        for h in range(heads):
            out[:, h * size : (h + 1) * size] = stacked[h * length : (h + 1) * length]
    v_ref[...] = jnp.dot(normed, weight_ref[2], preferred_element_type=F32).astype(BF16)
    scratch[...] = rows
    held_ref[...] = scratch[:, pl.ds(start, columns)].astype(BF16)
    gates = jnp.where(step, mod_ref[2, :, pl.ds(start, columns)], 0.0)
    gate_ref[...] = jnp.sum(gates, axis=0, keepdims=True)


def attend_kernel(q_ref, k_ref, v_ref, *refs, slots, tokens, stale, heads, size):
    old, outs = refs[:slots][::-1], refs[slots:]
    old = [r[: 2 * stale].astype(F32) for r in old]
    fresh_keys = k_ref[...].astype(F32)
    own = [slice(b * tokens, (b + 1) * tokens) for b in range(slots)]
    per = stale + tokens
    count = slots * per
    keys = jnp.concatenate([x for b in range(slots) for x in (old[b][:stale], fresh_keys[own[b]])], axis=0).astype(BF16)
    queries = q_ref[...]
    length = queries.shape[0]
    cuts = [slice(h * size, (h + 1) * size) for h in range(heads)]
    dims = (((1,), (1,)), ((), ()))
    scores = [lax.dot_general(queries[:, cut], keys[:, cut], dims, preferred_element_type=F32) for cut in cuts]
    fresh_values = v_ref[...].astype(F32)
    scores = jnp.concatenate(scores, axis=0) / math.sqrt(size)
    top = jnp.max(scores, axis=-1, keepdims=True)
    weights = jnp.exp(scores - top).astype(BF16).astype(F32)
    values = [x for b in range(slots) for x in (old[b][stale:], fresh_values[own[b]])]
    values = jnp.concatenate(values, axis=0).astype(BF16)
    lane = lax.broadcasted_iota(jnp.int32, weights.shape, 1)
    apart = [jnp.where((lane >= b * per) & (lane < (b + 1) * per), weights, 0.0).astype(BF16) for b in range(slots)]
    ones = jnp.ones((count, size), BF16)
    sums = []
    for h, cut in enumerate(cuts):
        rows = jnp.concatenate([x[h * length : (h + 1) * length] for x in apart], axis=0)
        extended = jnp.concatenate([values[:, cut], ones], axis=1)
        sums.append(jnp.dot(rows, extended, preferred_element_type=F32))
    rows = []
    for both in sums:
        both = both.astype(BF16).astype(F32)
        total = both[:length]
        for b in range(1, slots):
            total = total + both[b * length : (b + 1) * length]
        rows.append(total[:, :size] / total[:, size:])
    rows = jnp.concatenate(rows, axis=1)
    pieces = [rows[b * tokens : (b + 1) * tokens] for b in range(slots)]
    for b in range(slots):
        outs[b][:length] = swapped(pieces, b).astype(BF16)
        outs[b][length:] = jnp.concatenate([fresh_keys[own[b]], fresh_values[own[b]]], axis=0).astype(BF16)


def partial_kernel(weight_ref, *refs, numbers, rows, before):
    columns = weight_ref.shape[1]
    mine = lax.axis_index("seq")
    total = refs[len(numbers)][...] if before else None
    for ref, b in zip(refs[: len(numbers)], numbers, strict=True):
        start = pl.multiple_of((mine ^ b) * columns, columns)
        term = jnp.dot(ref[:rows], weight_ref[pl.ds(start, columns), :], preferred_element_type=F32)
        total = term if total is None else total + term
    refs[-1][...] = total


def peer(turn, section):
    mine = lax.axis_index("seq")
    entries = []
    for targets in turn:
        found = targets[0]
        for j in range(1, len(targets)):
            found = jnp.where(mine == j, targets[j], found)
        entries.append(found)
    return jnp.where(lax.rem(section, 2) == 0, entries[0], entries[1])


def output_kernel(gate_ref, held_ref, weight_ref, total_ref, attention_ref, *outs, number, tokens, turns):
    columns = weight_ref.shape[1]
    start = pl.multiple_of((lax.axis_index("seq") ^ number) * columns, columns)
    rows = total_ref.shape[0]
    total = total_ref[...] + jnp.dot(
        attention_ref[:rows], weight_ref[pl.ds(start, columns), :], preferred_element_type=F32
    )
    block = held_ref[...].astype(F32) + gate_ref[...] * total.astype(BF16).astype(F32)
    pieces = [block[b * tokens : (b + 1) * tokens] for b in range(len(outs))]
    mine = lax.axis_index("seq")
    for out, turn in zip(outs, turns, strict=True):
        slot = mine ^ peer(turn, lax.axis_index("section"))
        piece = pieces[0]
        for b in range(1, len(pieces)):
            piece = jnp.where(slot == b, pieces[b], piece)
        out[...] = piece.astype(BF16)


def place_kernel(*refs, slots, turns):
    out_ref, refs = refs[slots], refs[:slots][::-1]
    columns = refs[0].shape[1]
    sections = lax.axis_size("section")
    before = lax.rem(lax.axis_index("section") + (sections - 1), sections)
    for ref, turn in zip(refs, turns, strict=True):
        back = [[targets.index(j) for j in range(slots)] for targets in turn]
        start = pl.multiple_of(peer(back, before) * columns, columns)
        out_ref[0, :, pl.ds(start, columns)] = ref[...]


def place_kv_kernel(*refs, slots, tokens):
    out_ref, refs = refs[slots], refs[:slots][::-1]
    columns = refs[0].shape[1]
    mine = lax.axis_index("seq")
    for b in range(slots):
        start = pl.multiple_of((mine ^ b) * columns, columns)
        piece = refs[b][slots * tokens :].astype(F32)
        both = jnp.stack([piece[:tokens], piece[tokens:]], axis=1)
        out_ref[0, :, :, pl.ds(start, columns)] = both.astype(BF16)


def call(kernel, flops, out_shape, operands, scratch=(), **sizes):
    return pl.pallas_call(
        functools.partial(kernel, **sizes),
        out_shape=out_shape,
        in_specs=[VMEM] * len(operands),
        out_specs=jax.tree.map(lambda _: VMEM, out_shape),
        scratch_shapes=scratch,
        compiler_params=pltpu.CompilerParams(vmem_limit_bytes=16 * 2**20),
        cost_estimate=pl.CostEstimate(flops=int(flops), transcendentals=0, bytes_accessed=2**20),
    )(*operands)


def apart(slots):
    return APART if slots > 2 else ()


def body_by_heads(hidden, kv_cache, w_qkv, w_out, norm_gain, modulation, patch_order, timestep):
    slots, sections = lax.axis_size("seq"), lax.axis_size("section")
    tokens, width = hidden.shape[1:]
    patches = kv_cache.shape[1]
    columns, size = w_qkv.shape[3], norm_gain.shape[2]
    heads, stale, rows = columns // size, (patches - 1) * tokens, slots * tokens
    split = apart(slots)
    turns = TURNS if slots == 4 else [([j ^ b for j in range(slots)],) * 2 for b in range(slots)]

    def array(*shape, dtype=BF16):
        return jax.ShapeDtypeStruct(shape, dtype)

    def moved(array, number):
        return lax.ppermute(array, "seq", [(j, j ^ number) for j in range(slots)])

    def onward(array, number):
        turn = turns[number]
        pairs = [
            (j * sections + s, turn[s % 2][j] * sections + (s + 1) % sections)
            for j in range(slots)
            for s in range(sections)
        ]
        return lax.ppermute(array, ("seq", "section"), pairs)

    def exchanged(arrays):
        return [arrays[0]] + [moved(arrays[b], b) for b in range(1, slots)]

    own = hidden[0]
    alone = {b: moved(own, b) for b in split}
    ahead = call(ahead_kernel, 2e10, array(8, 128, dtype=F32), [])
    packed = {}
    far = tuple(b for b in range(1, slots) if b not in split)
    for numbers in (far, (0, *split)):
        outs = call(
            pack_kernel,
            5e9,
            [array(2 * stale + (rows if b in far else 0), columns) for b in numbers],
            [patch_order[None], ahead, own, kv_cache],
            numbers=numbers,
            slots=slots,
            patches=patches,
            columns=columns,
            split=split,
        )
        packed |= dict(zip(numbers, outs, strict=True))
    packed = [packed[b] for b in range(slots)]
    old = exchanged(packed)
    inputs = [own] + [alone[b] if b in split else old[b] for b in range(1, slots)]
    weights = jnp.transpose(w_qkv[0], (1, 0, 2))
    queries, keys, values, held, gate = call(
        project_kernel,
        2e9,
        [
            array(rows, columns),
            array(rows, columns),
            array(rows, columns),
            array(rows, columns),
            array(1, columns, dtype=F32),
        ],
        [timestep[None], jnp.transpose(modulation[0], (1, 0, 2)), norm_gain[0], weights, *inputs[::-1]],
        scratch=[pltpu.VMEM((rows, width), F32)],
        slots=slots,
        tokens=tokens,
        heads=heads,
        size=size,
        stale=stale,
    )
    ordered = call(
        attend_kernel,
        2e9,
        [array(rows + 2 * tokens, columns)] * slots,
        [queries, keys, values, *old[::-1]],
        slots=slots,
        tokens=tokens,
        stale=stale,
        heads=heads,
        size=size,
    )
    attention = exchanged(ordered)
    out_weights = w_out[0]
    groups = [(0, 2), (3,)] if slots == 4 else [(0,)] + [(b,) for b in range(slots - 1, 1, -1)]
    total = []
    for numbers in groups:
        operands = [out_weights] + [attention[b] for b in numbers] + total
        total = [
            call(
                partial_kernel,
                1e9,
                array(rows, columns, dtype=F32),
                operands,
                numbers=numbers,
                rows=rows,
                before=bool(total),
            )
        ]
    pieces = call(
        output_kernel,
        2e9,
        [array(tokens, columns)] * slots,
        [gate, held, out_weights, *total, attention[1]],
        number=1,
        tokens=tokens,
        turns=turns,
    )
    arrived = [onward(piece, number) for number, piece in enumerate(pieces)]
    fresh_kv = call(place_kv_kernel, 1e9, array(1, tokens, 2, width), attention[::-1], slots=slots, tokens=tokens)
    next_hidden = call(place_kernel, 1e9, array(1, tokens, width), arrived[::-1], slots=slots, turns=turns)
    return (next_hidden, fresh_kv)


def body_by_tokens(hidden, kv_cache, w_qkv, w_out, norm_gain, modulation, patch_order, timestep):
    section_index = lax.axis_index("section")
    patch_index = lax.dynamic_index_in_dim(patch_order, section_index, 0, keepdims=False)
    step_index = lax.dynamic_index_in_dim(timestep, section_index, 0, keepdims=False)
    modulate = lax.dynamic_index_in_dim(modulation[0], step_index, 0, keepdims=False)
    model_width = hidden.shape[2]
    head_size = norm_gain.shape[2]
    head_count = model_width // head_size
    col_width = w_qkv.shape[3]
    rows_in = hidden[0].astype(jnp.float32)
    own_count = rows_in.shape[0]
    normed = (layer_norm(rows_in) * (1.0 + modulate[1]) + modulate[0]).astype(jnp.bfloat16)
    w_local = w_qkv[0].reshape(model_width, 3 * col_width)
    projected = jnp.dot(
        lax.all_gather(normed, "seq", axis=0, tiled=True),
        w_local,
        preferred_element_type=jnp.float32,
    ).astype(jnp.bfloat16)
    patch_len = projected.shape[0]
    projected = projected.reshape(patch_len, 3, col_width)
    query_cols = lax.all_gather(projected[:, 0], "seq", axis=1, tiled=True)
    kv_rows = lax.all_to_all(projected[:, 1:], "seq", split_axis=0, concat_axis=2, tiled=True)
    queries = head_norm(
        query_cols.astype(jnp.float32).reshape(patch_len, head_count, head_size), norm_gain[0, 0]
    ).astype(jnp.bfloat16)
    key_rows = head_norm(
        kv_rows[:, 0].astype(jnp.float32).reshape(own_count, head_count, head_size), norm_gain[0, 1]
    ).astype(jnp.bfloat16)
    fresh = jnp.stack([key_rows.reshape(own_count, model_width), kv_rows[:, 1]], axis=1)
    zero = jnp.zeros((), jnp.int32)
    local_kv = lax.dynamic_update_slice(kv_cache[0], fresh[None], (patch_index, zero, zero, zero))
    patch_count = local_kv.shape[0]
    local_keys = local_kv[:, :, 0].reshape(patch_count * own_count, head_count, head_size)
    local_values = local_kv[:, :, 1].reshape(patch_count * own_count, head_count, head_size)
    scores = jnp.einsum(
        "thd,shd->hts", queries, local_keys, preferred_element_type=jnp.float32
    ) / math.sqrt(head_size)
    row_top = lax.pmax(jnp.max(scores, axis=-1), "seq")
    weights = jnp.exp(scores - row_top[:, :, None]).astype(jnp.bfloat16)
    denominator = jnp.sum(weights, axis=-1, dtype=jnp.float32).T
    numerator = jnp.einsum(
        "hts,shd->thd", weights, local_values, preferred_element_type=jnp.float32
    ).reshape(patch_len, model_width)
    totals, counts = (
        lax.psum(numerator.astype(jnp.bfloat16), "seq").astype(jnp.float32),
        lax.psum(denominator.astype(jnp.bfloat16), "seq").astype(jnp.float32),
    )
    attention = (totals.reshape(patch_len, head_count, head_size) / counts[:, :, None]).astype(
        jnp.bfloat16
    )
    attention = attention.reshape(patch_len, model_width)
    out_cols = jnp.dot(attention, w_out[0], preferred_element_type=jnp.float32).astype(jnp.bfloat16)
    out_rows = lax.all_to_all(out_cols, "seq", split_axis=0, concat_axis=1, tiled=True)
    block = (rows_in + modulate[2] * out_rows.astype(jnp.float32)).astype(jnp.bfloat16)
    arrived = passed_along(block, "section", 1)
    return (arrived[None], fresh[None])


def body(hidden, kv_cache, w_qkv, w_out, norm_gain, modulation, patch_order, timestep):
    count = lax.axis_size("seq")
    whole_heads = w_qkv.shape[3] % norm_gain.shape[2] == 0
    chosen = body_by_heads if whole_heads and count & (count - 1) == 0 else body_by_tokens
    return chosen(hidden, kv_cache, w_qkv, w_out, norm_gain, modulation, patch_order, timestep)


def solution(mesh):
    return jax.shard_map(
        body,
        mesh=mesh,
        in_specs=(
            P("section", ("groups", "seq"), None),
            P("section", None, ("groups", "seq"), None, None),
            P("section", None, None, "seq"),
            P("section", None, "seq"),
            P("section", None, None),
            P("section", None, None, None),
            P("groups"),
            P("groups"),
        ),
        out_specs=(
            P("section", ("groups", "seq"), None),
            P("section", ("groups", "seq"), None, None),
        ),
        check_vma=False,
    )
```

```python
import functools
import math

import jax
import jax.numpy as jnp
from jax import lax
from jax.experimental import pallas as pl
from jax.experimental.pallas import tpu as pltpu
from jax.sharding import PartitionSpec as P


APART = (1, 2)
TURNS = (
    ((2, 3, 1, 0), (1, 2, 0, 3)),
    ((1, 0, 3, 2), (2, 3, 1, 0)),
    ((0, 1, 2, 3), (0, 1, 3, 2)),
    ((3, 2, 0, 1), (3, 0, 2, 1)),
)

F32 = jnp.float32
BF16 = jnp.bfloat16
VMEM = pl.BlockSpec(memory_space=pltpu.VMEM)


def passed_along(array, axis, by):
    count = lax.axis_size(axis)
    return lax.ppermute(array, axis, [(i, (i + by) % count) for i in range(count)])


def layer_norm(values_in):
    center = values_in - jnp.mean(values_in, axis=-1, keepdims=True)
    spread = jnp.mean(center * center, axis=-1, keepdims=True)
    return center * lax.rsqrt(spread + 1e-06)


def head_norm(values_in, gain):
    square = jnp.mean(values_in * values_in, axis=-1, keepdims=True)
    return values_in * lax.rsqrt(square + 1e-06) * gain


def swapped(slots, number):
    return jnp.concatenate([slots[b ^ number] for b in range(len(slots))], axis=0)


def ahead_kernel(out_ref):
    out_ref[...] = jnp.zeros_like(out_ref)


def entry(ref):
    lane = lax.broadcasted_iota(jnp.int32, ref.shape, 1)
    mine = lane == lax.axis_index("section")
    return jnp.sum(jnp.where(mine, ref[...], 0).astype(F32), axis=1, keepdims=True)


def pack_kernel(order_ref, _, hidden_ref, cache_ref, *outs, numbers, slots, patches, columns, split):
    mine = lax.axis_index("seq")
    patch = entry(order_ref)
    for out, b in zip(outs, numbers, strict=True):
        start = pl.multiple_of((mine ^ b) * columns, columns)
        both = [cache_ref[0, p, :, :, pl.ds(start, columns)].astype(F32) for p in range(patches)]
        both = [x[:, part] for part in range(2) for x in both]
        stale = []
        for part in range(2):
            for i in range(part * patches, (part + 1) * patches - 1):
                stale.append(jnp.where(patch > i - part * patches, both[i], both[i + 1]))
        stale = jnp.concatenate(stale, axis=0).astype(BF16)
        out[: stale.shape[0]] = stale
        if b and b not in split:
            hidden = hidden_ref[...].astype(F32)
            hidden = [hidden[:, c * columns : (c + 1) * columns] for c in range(slots)]
            out[stale.shape[0] :] = jnp.concatenate(hidden, axis=0).astype(BF16)


def project_kernel(step_ref, mod_ref, gain_ref, weight_ref, *refs, slots, tokens, heads, size, stale):
    hidden_refs = refs[:slots][::-1]
    q_ref, k_ref, v_ref, held_ref, gate_ref, scratch = refs[slots:]
    mine = lax.axis_index("seq")
    columns, length = heads * size, slots * tokens
    step = lax.broadcasted_iota(jnp.int32, (mod_ref.shape[1], 1), 0).astype(F32) == entry(step_ref)
    modulate = [jnp.sum(jnp.where(step, mod_ref[i], 0.0), axis=0, keepdims=True) for i in range(2)]
    start = pl.multiple_of(mine * columns, columns)
    rows = []
    for ref in hidden_refs:
        if ref.shape[0] == tokens:
            rows.append(ref[...].astype(F32))
        else:
            cut = ref[2 * stale :].astype(F32)
            rows.append(jnp.concatenate([cut[c * tokens : (c + 1) * tokens] for c in range(slots)], axis=1))
    rows = jnp.concatenate(rows, axis=0)
    normed = (layer_norm(rows) * (1.0 + modulate[1]) + modulate[0]).astype(BF16)
    for part, out in enumerate((q_ref, k_ref)):
        dotted = jnp.dot(normed, weight_ref[part], preferred_element_type=F32).astype(BF16).astype(F32)
        stacked = jnp.concatenate([dotted[:, h * size : (h + 1) * size] for h in range(heads)], axis=0)
        stacked = head_norm(stacked, gain_ref[pl.ds(part, 1), :]).astype(BF16)
        for h in range(heads):
            out[:, h * size : (h + 1) * size] = stacked[h * length : (h + 1) * length]
    v_ref[...] = jnp.dot(normed, weight_ref[2], preferred_element_type=F32).astype(BF16)
    scratch[...] = rows
    held_ref[...] = scratch[:, pl.ds(start, columns)].astype(BF16)
    gates = jnp.where(step, mod_ref[2, :, pl.ds(start, columns)], 0.0)
    gate_ref[...] = jnp.sum(gates, axis=0, keepdims=True)


def attend_kernel(q_ref, k_ref, v_ref, *refs, slots, tokens, stale, heads, size):
    old, outs = refs[:slots][::-1], refs[slots:]
    old = [r[: 2 * stale].astype(F32) for r in old]
    fresh_keys = k_ref[...].astype(F32)
    own = [slice(b * tokens, (b + 1) * tokens) for b in range(slots)]
    per = stale + tokens
    count = slots * per
    keys = jnp.concatenate([x for b in range(slots) for x in (old[b][:stale], fresh_keys[own[b]])], axis=0).astype(BF16)
    queries = q_ref[...]
    length = queries.shape[0]
    cuts = [slice(h * size, (h + 1) * size) for h in range(heads)]
    dims = (((1,), (1,)), ((), ()))
    scores = [lax.dot_general(queries[:, cut], keys[:, cut], dims, preferred_element_type=F32) for cut in cuts]
    fresh_values = v_ref[...].astype(F32)
    scores = jnp.concatenate(scores, axis=0) / math.sqrt(size)
    top = jnp.max(scores, axis=-1, keepdims=True)
    weights = jnp.exp(scores - top).astype(BF16).astype(F32)
    values = [x for b in range(slots) for x in (old[b][stale:], fresh_values[own[b]])]
    values = jnp.concatenate(values, axis=0).astype(BF16)
    lane = lax.broadcasted_iota(jnp.int32, weights.shape, 1)
    apart = [jnp.where((lane >= b * per) & (lane < (b + 1) * per), weights, 0.0).astype(BF16) for b in range(slots)]
    ones = jnp.ones((count, size), BF16)
    sums = []
    for h, cut in enumerate(cuts):
        rows = jnp.concatenate([x[h * length : (h + 1) * length] for x in apart], axis=0)
        extended = jnp.concatenate([values[:, cut], ones], axis=1)
        sums.append(jnp.dot(rows, extended, preferred_element_type=F32))
    rows = []
    for both in sums:
        both = both.astype(BF16).astype(F32)
        total = both[:length]
        for b in range(1, slots):
            total = total + both[b * length : (b + 1) * length]
        rows.append(total[:, :size] / total[:, size:])
    rows = jnp.concatenate(rows, axis=1)
    pieces = [rows[b * tokens : (b + 1) * tokens] for b in range(slots)]
    for b in range(slots):
        outs[b][:length] = swapped(pieces, b).astype(BF16)
        outs[b][length:] = jnp.concatenate([fresh_keys[own[b]], fresh_values[own[b]]], axis=0).astype(BF16)


def partial_kernel(weight_ref, *refs, numbers, rows, before):
    columns = weight_ref.shape[1]
    mine = lax.axis_index("seq")
    total = refs[len(numbers)][...] if before else None
    for ref, b in zip(refs[: len(numbers)], numbers, strict=True):
        start = pl.multiple_of((mine ^ b) * columns, columns)
        term = jnp.dot(ref[:rows], weight_ref[pl.ds(start, columns), :], preferred_element_type=F32)
        total = term if total is None else total + term
    refs[-1][...] = total


def peer(turn, section):
    mine = lax.axis_index("seq")
    entries = []
    for targets in turn:
        found = targets[0]
        for j in range(1, len(targets)):
            found = jnp.where(mine == j, targets[j], found)
        entries.append(found)
    return jnp.where(lax.rem(section, 2) == 0, entries[0], entries[1])


def output_kernel(gate_ref, held_ref, weight_ref, total_ref, attention_ref, *outs, number, tokens, turns):
    columns = weight_ref.shape[1]
    start = pl.multiple_of((lax.axis_index("seq") ^ number) * columns, columns)
    rows = total_ref.shape[0]
    total = total_ref[...] + jnp.dot(
        attention_ref[:rows], weight_ref[pl.ds(start, columns), :], preferred_element_type=F32
    )
    block = held_ref[...].astype(F32) + gate_ref[...] * total.astype(BF16).astype(F32)
    pieces = [block[b * tokens : (b + 1) * tokens] for b in range(len(outs))]
    mine = lax.axis_index("seq")
    for out, turn in zip(outs, turns, strict=True):
        slot = mine ^ peer(turn, lax.axis_index("section"))
        piece = pieces[0]
        for b in range(1, len(pieces)):
            piece = jnp.where(slot == b, pieces[b], piece)
        out[...] = piece.astype(BF16)


def place_kernel(*refs, slots, turns):
    out_ref, refs = refs[slots], refs[:slots][::-1]
    columns = refs[0].shape[1]
    sections = lax.axis_size("section")
    before = lax.rem(lax.axis_index("section") + (sections - 1), sections)
    for ref, turn in zip(refs, turns, strict=True):
        back = [[targets.index(j) for j in range(slots)] for targets in turn]
        start = pl.multiple_of(peer(back, before) * columns, columns)
        out_ref[0, :, pl.ds(start, columns)] = ref[...]


def place_kv_kernel(*refs, slots, tokens):
    out_ref, refs = refs[slots], refs[:slots][::-1]
    columns = refs[0].shape[1]
    mine = lax.axis_index("seq")
    for b in range(slots):
        start = pl.multiple_of((mine ^ b) * columns, columns)
        piece = refs[b][slots * tokens :].astype(F32)
        both = jnp.stack([piece[:tokens], piece[tokens:]], axis=1)
        out_ref[0, :, :, pl.ds(start, columns)] = both.astype(BF16)


def call(kernel, flops, out_shape, operands, scratch=(), **sizes):
    return pl.pallas_call(
        functools.partial(kernel, **sizes),
        out_shape=out_shape,
        in_specs=[VMEM] * len(operands),
        out_specs=jax.tree.map(lambda _: VMEM, out_shape),
        scratch_shapes=scratch,
        compiler_params=pltpu.CompilerParams(vmem_limit_bytes=16 * 2**20),
        cost_estimate=pl.CostEstimate(flops=int(flops), transcendentals=0, bytes_accessed=2**20),
    )(*operands)


def apart(slots):
    return APART if slots > 2 else ()


def body_by_heads(hidden, kv_cache, w_qkv, w_out, norm_gain, modulation, patch_order, timestep):
    slots, sections = lax.axis_size("seq"), lax.axis_size("section")
    tokens, width = hidden.shape[1:]
    patches = kv_cache.shape[1]
    columns, size = w_qkv.shape[3], norm_gain.shape[2]
    heads, stale, rows = columns // size, (patches - 1) * tokens, slots * tokens
    split = apart(slots)
    turns = TURNS if slots == 4 else [([j ^ b for j in range(slots)],) * 2 for b in range(slots)]

    def array(*shape, dtype=BF16):
        return jax.ShapeDtypeStruct(shape, dtype)

    def moved(array, number):
        return lax.ppermute(array, "seq", [(j, j ^ number) for j in range(slots)])

    def onward(array, number):
        turn = turns[number]
        pairs = [
            (j * sections + s, turn[s % 2][j] * sections + (s + 1) % sections)
            for j in range(slots)
            for s in range(sections)
        ]
        return lax.ppermute(array, ("seq", "section"), pairs)

    def exchanged(arrays):
        return [arrays[0]] + [moved(arrays[b], b) for b in range(1, slots)]

    own = hidden[0]
    alone = {b: moved(own, b) for b in split}
    ahead = call(ahead_kernel, 5e9, array(8, 128, dtype=F32), [])
    packed = {}
    far = tuple(b for b in range(1, slots) if b not in split)
    for numbers in (far, (0, *split)):
        outs = call(
            pack_kernel,
            5e9,
            [array(2 * stale + (rows if b in far else 0), columns) for b in numbers],
            [patch_order[None], ahead, own, kv_cache],
            numbers=numbers,
            slots=slots,
            patches=patches,
            columns=columns,
            split=split,
        )
        packed |= dict(zip(numbers, outs, strict=True))
    packed = [packed[b] for b in range(slots)]
    old = exchanged(packed)
    inputs = [own] + [alone[b] if b in split else old[b] for b in range(1, slots)]
    weights = jnp.transpose(w_qkv[0], (1, 0, 2))
    queries, keys, values, held, gate = call(
        project_kernel,
        2e9,
        [
            array(rows, columns),
            array(rows, columns),
            array(rows, columns),
            array(rows, columns),
            array(1, columns, dtype=F32),
        ],
        [timestep[None], jnp.transpose(modulation[0], (1, 0, 2)), norm_gain[0], weights, *inputs[::-1]],
        scratch=[pltpu.VMEM((rows, width), F32)],
        slots=slots,
        tokens=tokens,
        heads=heads,
        size=size,
        stale=stale,
    )
    ordered = call(
        attend_kernel,
        2e9,
        [array(rows + 2 * tokens, columns)] * slots,
        [queries, keys, values, *old[::-1]],
        slots=slots,
        tokens=tokens,
        stale=stale,
        heads=heads,
        size=size,
    )
    attention = exchanged(ordered)
    out_weights = w_out[0]
    groups = [(0, 2), (3,)] if slots == 4 else [(0,)] + [(b,) for b in range(slots - 1, 1, -1)]
    total = []
    for numbers in groups:
        operands = [out_weights] + [attention[b] for b in numbers] + total
        total = [
            call(
                partial_kernel,
                1e9,
                array(rows, columns, dtype=F32),
                operands,
                numbers=numbers,
                rows=rows,
                before=bool(total),
            )
        ]
    pieces = call(
        output_kernel,
        2e9,
        [array(tokens, columns)] * slots,
        [gate, held, out_weights, *total, attention[1]],
        number=1,
        tokens=tokens,
        turns=turns,
    )
    arrived = [onward(piece, number) for number, piece in enumerate(pieces)]
    fresh_kv = call(place_kv_kernel, 1e9, array(1, tokens, 2, width), attention[::-1], slots=slots, tokens=tokens)
    next_hidden = call(place_kernel, 1e9, array(1, tokens, width), arrived[::-1], slots=slots, turns=turns)
    return (next_hidden, fresh_kv)


def body_by_tokens(hidden, kv_cache, w_qkv, w_out, norm_gain, modulation, patch_order, timestep):
    section_index = lax.axis_index("section")
    patch_index = lax.dynamic_index_in_dim(patch_order, section_index, 0, keepdims=False)
    step_index = lax.dynamic_index_in_dim(timestep, section_index, 0, keepdims=False)
    modulate = lax.dynamic_index_in_dim(modulation[0], step_index, 0, keepdims=False)
    model_width = hidden.shape[2]
    head_size = norm_gain.shape[2]
    head_count = model_width // head_size
    col_width = w_qkv.shape[3]
    rows_in = hidden[0].astype(jnp.float32)
    own_count = rows_in.shape[0]
    normed = (layer_norm(rows_in) * (1.0 + modulate[1]) + modulate[0]).astype(jnp.bfloat16)
    w_local = w_qkv[0].reshape(model_width, 3 * col_width)
    projected = jnp.dot(
        lax.all_gather(normed, "seq", axis=0, tiled=True),
        w_local,
        preferred_element_type=jnp.float32,
    ).astype(jnp.bfloat16)
    patch_len = projected.shape[0]
    projected = projected.reshape(patch_len, 3, col_width)
    query_cols = lax.all_gather(projected[:, 0], "seq", axis=1, tiled=True)
    kv_rows = lax.all_to_all(projected[:, 1:], "seq", split_axis=0, concat_axis=2, tiled=True)
    queries = head_norm(
        query_cols.astype(jnp.float32).reshape(patch_len, head_count, head_size), norm_gain[0, 0]
    ).astype(jnp.bfloat16)
    key_rows = head_norm(
        kv_rows[:, 0].astype(jnp.float32).reshape(own_count, head_count, head_size), norm_gain[0, 1]
    ).astype(jnp.bfloat16)
    fresh = jnp.stack([key_rows.reshape(own_count, model_width), kv_rows[:, 1]], axis=1)
    zero = jnp.zeros((), jnp.int32)
    local_kv = lax.dynamic_update_slice(kv_cache[0], fresh[None], (patch_index, zero, zero, zero))
    patch_count = local_kv.shape[0]
    local_keys = local_kv[:, :, 0].reshape(patch_count * own_count, head_count, head_size)
    local_values = local_kv[:, :, 1].reshape(patch_count * own_count, head_count, head_size)
    scores = jnp.einsum(
        "thd,shd->hts", queries, local_keys, preferred_element_type=jnp.float32
    ) / math.sqrt(head_size)
    row_top = lax.pmax(jnp.max(scores, axis=-1), "seq")
    weights = jnp.exp(scores - row_top[:, :, None]).astype(jnp.bfloat16)
    denominator = jnp.sum(weights, axis=-1, dtype=jnp.float32).T
    numerator = jnp.einsum(
        "hts,shd->thd", weights, local_values, preferred_element_type=jnp.float32
    ).reshape(patch_len, model_width)
    totals, counts = (
        lax.psum(numerator.astype(jnp.bfloat16), "seq").astype(jnp.float32),
        lax.psum(denominator.astype(jnp.bfloat16), "seq").astype(jnp.float32),
    )
    attention = (totals.reshape(patch_len, head_count, head_size) / counts[:, :, None]).astype(
        jnp.bfloat16
    )
    attention = attention.reshape(patch_len, model_width)
    out_cols = jnp.dot(attention, w_out[0], preferred_element_type=jnp.float32).astype(jnp.bfloat16)
    out_rows = lax.all_to_all(out_cols, "seq", split_axis=0, concat_axis=1, tiled=True)
    block = (rows_in + modulate[2] * out_rows.astype(jnp.float32)).astype(jnp.bfloat16)
    arrived = passed_along(block, "section", 1)
    return (arrived[None], fresh[None])


def body(hidden, kv_cache, w_qkv, w_out, norm_gain, modulation, patch_order, timestep):
    count = lax.axis_size("seq")
    whole_heads = w_qkv.shape[3] % norm_gain.shape[2] == 0
    chosen = body_by_heads if whole_heads and count & (count - 1) == 0 else body_by_tokens
    return chosen(hidden, kv_cache, w_qkv, w_out, norm_gain, modulation, patch_order, timestep)


def solution(mesh):
    return jax.shard_map(
        body,
        mesh=mesh,
        in_specs=(
            P("section", ("groups", "seq"), None),
            P("section", None, ("groups", "seq"), None, None),
            P("section", None, None, "seq"),
            P("section", None, "seq"),
            P("section", None, None),
            P("section", None, None, None),
            P("groups"),
            P("groups"),
        ),
        out_specs=(
            P("section", ("groups", "seq"), None),
            P("section", ("groups", "seq"), None, None),
        ),
        check_vma=False,
    )
```
